32 devices in a mesh: width: 8 (over z, x), thick: 4 (over y, core).
Axes of the slice: x: 2, y: 2, z: 4, core: 2. Of those that a mesh axis runs over, the one named last changes fastest.
Arguments:
- deviation: float32 [6, 16, 64, 1024], P(None, 'thick', 'width'), may hold values from -4.6 to 4.6, as said below
- velocity: float32 [3, 16, 64, 1024], P(None, 'thick', 'width'), may hold values from -4 to 4
- stiffness: float32 [16, 64, 1024], P('thick', 'width'), may hold values from 0.1 to 16, as said below
Outputs:
- deviation_next: float32 [6, 16, 64, 1024], P(None, 'thick', 'width')
- solution: float32 [3, 16, 64, 1024], P(None, 'thick', 'width')
The draws below stay inside these ranges and needn't reach their ends.
Inputs may be any that keep to these rules, and one draw needn't show every extreme that they name: `deviation`: entries are independent across cells. `stiffness`: positive at every node.
All inputs are finite; a program needn't handle non-finite values.
Results may differ from the reference program's by a relative error of at most 0.0019.
Values sent between devices are 32-bit elements; how exact they have to be, the bound alone decides.
No kernel may reach another device: no remote copies, remote signals or barrier semaphores. Data moves between devices by JAX's collectives and lax.ppermute only.
A program may use at most 64 MiB of HBM per device.

```python
import jax
import jax.numpy as jnp
from jax import lax

NL = 1024
ITERS = 2
NT = 16
NW = 64


def draw_deviation(key, part):
    across = jnp.arange(NW, dtype=jnp.float32) / NW
    rough = jnp.clip(jax.random.normal(key, (6, NT, NW, NL), jnp.float32), -4.0, 4.0)
    ramp = 1.0 + 2.0 * across
    return 0.3 * rough * ramp[None, None, :, None]


def draw_stiffness(key, part):
    across = jnp.arange(NW, dtype=jnp.float32) / NW
    rough = jnp.exp(jax.random.uniform(key, (NT, NW, NL), jnp.float32, -0.7, 0.7))
    profile = 0.3 * 10.0 ** across
    return rough * profile[None, :, None]


def shard_levels(key, shape, cuts, low, top_value):
    level, own = 1.0, jax.random.fold_in(key, 6)
    for axis_at, shards_of in cuts:
        draws = jnp.exp(jax.random.uniform(jax.random.fold_in(own, axis_at), (shards_of,), jnp.float32, low / len(cuts), top_value / len(cuts)))
        level = level * jnp.repeat(draws, shape[axis_at] // shards_of).reshape([-1 if axis == axis_at else 1 for axis in range(len(shape))])
    return level


def normal_values(key, dims, width, reach, shards=(), held_as=jnp.bfloat16):
    values = jax.random.normal(key, dims, jnp.float32) * width
    if len(shards) > 0:
        values = shard_levels(key, dims, shards, -0.22, 0.18) * values
    return jnp.clip(values, min=-reach, max=reach).astype(held_as)


def setup_inputs(seed: int = 0) -> dict:
    streams_of = jax.random.split(jax.random.key(seed), 4)
    deviation = draw_deviation(jax.random.fold_in(streams_of[3], 71), 0)
    velocity = normal_values(streams_of[1], (3, NT, NW, NL), 1.0, 4.0, ((1, 4), (2, 8)), jnp.float32)
    stiffness = draw_stiffness(jax.random.fold_in(streams_of[3], 71), 0)
    return {"deviation": deviation, "velocity": velocity, "stiffness": stiffness}


TIME_STEP = 0.1
RELAX_TIME = 1.0
MOBILITY = 0.3
MODULUS = 10.0
pair_table = ((0, 0), (1, 1), (2, 2), (0, 1), (0, 2), (1, 2))
slot_table = ((0, 3, 4), (3, 1, 5), (4, 5, 2))


def advance(padded):
    padded = jnp.pad(padded, ((0, 0), (0, 0), (0, 0), (1, 1)))
    extent = (padded.shape[1] - 2, padded.shape[2] - 2, padded.shape[3] - 2)

    def neighbour(axis_dim, offset):
        starts = [1, 1, 1]
        starts[axis_dim] += offset
        return padded[:, starts[0]:starts[0] + extent[0], starts[1]:starts[1] + extent[1], starts[2]:starts[2] + extent[2]]

    centre = neighbour(0, 0)
    beneath = [neighbour(d, -1) for d in range(3)]
    above_cells = [neighbour(d, 1) for d in range(3)]
    gradient = [[0.5 * (above_cells[j][6 + i] - beneath[j][6 + i]) for j in range(3)] for i in range(3)]
    tensor = [[centre[slot_table[i][j]] for j in range(3)] for i in range(3)]
    changes = []
    for p in range(6):
        i, j = pair_table[p]
        advected = jnp.zeros_like(centre[p])
        for d in range(3):
            flow_speed = centre[6 + d]
            advected = advected + jnp.maximum(flow_speed, 0.0) * (centre[p] - beneath[d][p]) + jnp.minimum(flow_speed, 0.0) * (above_cells[d][p] - centre[p])
        stretch = sum(gradient[i][k] * tensor[k][j] + gradient[j][k] * tensor[k][i] for k in range(3))
        square = sum(tensor[i][k] * tensor[k][j] for k in range(3))
        change = -advected + gradient[i][j] + gradient[j][i] + stretch - (centre[p] + MOBILITY * square) / RELAX_TIME
        changes.append(centre[p] + TIME_STEP * change)
    return jnp.stack(changes)


def pair_sum(values, axis_dim):
    reduced = values.shape[axis_dim] - 1
    return lax.slice_in_dim(values, 1, reduced + 1, axis=axis_dim) + lax.slice_in_dim(values, 0, reduced, axis=axis_dim)


def pair_diff(values, axis_dim):
    reduced = values.shape[axis_dim] - 1
    return lax.slice_in_dim(values, 1, reduced + 1, axis=axis_dim) - lax.slice_in_dim(values, 0, reduced, axis=axis_dim)


def assemble(stress):
    stress = jnp.pad(stress, ((0, 0), (0, 0), (0, 0), (1, 0)))
    result = []
    for i in range(3):
        summed = None
        for d in range(3):
            member = stress[slot_table[i][d]]
            for e in range(3):
                member = pair_diff(member, e) if e == d else pair_sum(member, e)
            summed = member if summed is None else summed + member
        result.append(summed)
    return (0.25 * MODULUS) * jnp.stack(result)


def operate(nodal, stiffness):
    padded = jnp.pad(nodal, ((0, 0), (1, 1), (1, 1), (1, 1)))
    beside = padded[:, 2:, 1:-1, 1:-1] + padded[:, :-2, 1:-1, 1:-1]
    beside = beside + padded[:, 1:-1, 2:, 1:-1] + padded[:, 1:-1, :-2, 1:-1]
    beside = beside + padded[:, 1:-1, 1:-1, 2:] + padded[:, 1:-1, 1:-1, :-2]
    return (6.0 + stiffness)[None] * nodal - beside


def reference(deviation, velocity, stiffness):
    stacked = jnp.concatenate([deviation, velocity], axis=0)
    padded = jnp.pad(stacked, ((0, 0), (1, 1), (1, 1), (0, 0)))

    def one_layer(layer_index):
        window = lax.dynamic_slice_in_dim(padded, layer_index, 3, axis=1)
        return advance(window)[:, 0]

    layered = lax.map(one_layer, jnp.arange(NT, dtype=jnp.int32))
    deviation_next = jnp.moveaxis(layered, 0, 1)
    forces = assemble(jnp.pad(deviation_next, ((0, 0), (1, 0), (1, 0), (0, 0))))
    solution = jnp.zeros_like(forces)
    residual = forces
    direction = forces
    norm_now = jnp.sum(residual * residual)
    for iterate in range(ITERS):
        mapped = operate(direction, stiffness)
        step_size = norm_now / jnp.sum(direction * mapped)
        solution = solution + step_size * direction
        if iterate + 1 < ITERS:
            residual = residual - step_size * mapped
            norm_next = jnp.sum(residual * residual)
            direction = residual + (norm_next / norm_now) * direction
            norm_now = norm_next
    return deviation_next, solution
```

```python
import functools

import jax
import jax.numpy as jnp
from jax import lax
from jax.experimental import pallas as pl
from jax.experimental.pallas import tpu as pltpu
from jax.sharding import PartitionSpec as P

TIME_STEP = 0.1
RELAX_TIME = 1.0
MOBILITY = 0.3
MODULUS = 10.0
LANES = 128
AXES = ("width", "thick")
PAIRS = ((0, 0), (1, 1), (2, 2), (0, 1), (0, 2), (1, 2))
SLOT = ((0, 3, 4), (3, 1, 5), (4, 5, 2))
VMEM_LIMIT = 40 * 1024 * 1024


def swap_pairs(wide, thick):
    def flat(fn):
        return [
            (w * thick + t, fn(w, t)[0] * thick + fn(w, t)[1])
            for w in range(wide)
            for t in range(thick)
        ]

    def width_second(w, t):
        return (w, t ^ 1) if w in (0, wide - 1) else (((w - 1) ^ 1) + 1, t)

    def thick_second(w, t):
        return (w ^ 2, t) if t in (0, thick - 1) else (w, ((t - 1) ^ 1) + 1)

    return (
        flat(lambda w, t: (w ^ 1, t)),
        flat(width_second),
        flat(lambda w, t: (w, t ^ 1)),
        flat(thick_second),
    )


def swap(value, pairs):
    return lax.ppermute(value, AXES, pairs)


def as_tiles(x):
    *lead, w, length = x.shape
    x = x.reshape(*lead, w, length // LANES, LANES)
    return jnp.swapaxes(x, -3, -2).reshape(*lead, length // LANES * w, LANES)


def from_tiles(x, w):
    *lead, rows, lanes = x.shape
    x = x.reshape(*lead, rows // w, w, lanes)
    return jnp.swapaxes(x, -3, -2).reshape(*lead, w, rows // w * lanes)


def row_of(ref, lead, w, columns, sub):
    return ref[(*lead, pl.ds(w, sub, stride=columns), slice(None))]


def edge_masks(sub):
    lane = lax.broadcasted_iota(jnp.int32, (sub, LANES), 1)
    row = lax.broadcasted_iota(jnp.int32, (sub, LANES), 0)
    first, last = lane == 0, lane == LANES - 1
    return first, first & (row == 0), last, last & (row == sub - 1)


def before(x, masks):
    first, corner = masks[0], masks[1]
    near = pltpu.roll(x, 1, axis=1)
    far = pltpu.roll(near, 1, axis=0)
    return jnp.where(corner, 0.0, jnp.where(first, far, near))


def after(x, masks):
    last, corner = masks[2], masks[3]
    sub = x.shape[0]
    near = pltpu.roll(x, LANES - 1, axis=1)
    far = pltpu.roll(near, sub - 1, axis=0)
    return jnp.where(corner, 0.0, jnp.where(last, far, near))


def place():
    w, t = lax.axis_index("width"), lax.axis_index("thick")
    return w, t, w % 2 == 0, t % 2 == 0


def pack_kernel(dims, dev, vel, stiff, wa, wb, ta, tb):
    layers, columns, sub = dims
    _, _, w_even, t_even = place()

    def source(c):
        if c < 6:
            return dev, (c,)
        if c < 9:
            return vel, (c - 6,)
        return stiff, ()

    for c in range(10):
        ref, lead = source(c)
        for t in range(layers):
            low = row_of(ref, (*lead, t), 0, columns, sub)
            high = row_of(ref, (*lead, t), columns - 1, columns, sub)
            wa[c, t] = jnp.where(w_even, high, low)
            wb[c, t] = jnp.where(w_even, low, high)
        bottom = ref[(*lead, 0)]
        top = ref[(*lead, layers - 1)]
        ta[c] = jnp.where(t_even, top, bottom)
        tb[c] = jnp.where(t_even, bottom, top)


def advance_kernel(
    dims, ends, dev, vel, wa, wb, ta, tb, new, part, sa, sb, ext, tau
):
    layers, columns, sub = dims
    w_at, t_at, w_even, t_even = place()
    masks = edge_masks(sub)
    zero = jnp.zeros((sub, LANES), jnp.float32)
    w_low, w_high = w_at > 0, w_at < ends[0] - 1
    t_low, t_high = t_at > 0, t_at < ends[1] - 1

    for c in range(9):
        ref, lead = (dev, (c,)) if c < 6 else (vel, (c - 6,))
        for t in range(layers):
            for w in range(columns):
                ext[c, t + 1, w + 1] = row_of(ref, (*lead, t), w, columns, sub)
            a, b = wa[c, t], wb[c, t]
            ext[c, t + 1, 0] = jnp.where(w_low, jnp.where(w_even, b, a), zero)
            ext[c, t + 1, columns + 1] = jnp.where(w_high, jnp.where(w_even, a, b), zero)
        for w in range(columns):
            a = row_of(ta, (c,), w, columns, sub)
            b = row_of(tb, (c,), w, columns, sub)
            ext[c, 0, w + 1] = jnp.where(t_low, jnp.where(t_even, b, a), zero)
            ext[c, layers + 1, w + 1] = jnp.where(t_high, jnp.where(t_even, a, b), zero)

    def cell(t, w):
        def at(c, d, off):
            where = [t + 1, w + 1]
            where[d] = where[d] + off
            return ext[c, where[0], where[1]]

        s = [ext[c, t + 1, w + 1] for c in range(6)]
        u = [ext[6 + c, t + 1, w + 1] for c in range(3)]
        half = 0.5 * TIME_STEP
        grad = [
            [half * (at(6 + i, j, 1) - at(6 + i, j, -1)) for j in range(2)]
            + [half * (after(u[i], masks) - before(u[i], masks))]
            for i in range(3)
        ]
        pos = [TIME_STEP * jnp.maximum(u[d], 0.0) for d in range(3)]
        neg = [TIME_STEP * jnp.minimum(u[d], 0.0) for d in range(3)]
        keep = (1.0 - TIME_STEP / RELAX_TIME) - (
            (pos[0] - neg[0]) + (pos[1] - neg[1]) + (pos[2] - neg[2])
        )
        bend = 0.5 * TIME_STEP * MOBILITY / RELAX_TIME
        scaled = [bend * s[c] for c in range(6)]
        turn = [[grad[i][k] - scaled[SLOT[i][k]] for k in range(3)] for i in range(3)]
        for p, (i, j) in enumerate(PAIRS):
            out = keep * s[p]
            for d in range(2):
                out = out + pos[d] * at(p, d, -1) - neg[d] * at(p, d, 1)
            out = out + pos[2] * before(s[p], masks) - neg[2] * after(s[p], masks)
            if i == j:
                more = grad[i][i]
                for k in range(3):
                    more = more + turn[i][k] * s[SLOT[k][i]]
                out = out + 2.0 * more
            else:
                out = out + (grad[i][j] + grad[j][i])
                for k in range(3):
                    out = out + turn[i][k] * s[SLOT[k][j]] + turn[j][k] * s[SLOT[k][i]]
            tau[p, t, w] = out

    def cells(step, carry):
        t, w = step // (columns // 2), step % (columns // 2)
        cell(t, 2 * w)
        cell(t, 2 * w + 1)
        return carry

    lax.fori_loop(0, layers * columns // 2, cells, 0)

    scale = 0.25 * MODULUS

    def column(w, carry):
        lower = None
        for t in range(layers + 1):
            plus = minus = None
            if t < layers:
                here = [tau[c, t, jnp.minimum(w, columns - 1)] for c in range(6)]
                back = [tau[c, t, jnp.maximum(w - 1, 0)] for c in range(6)]
                here = [jnp.where(w < columns, x, zero) for x in here]
                back = [jnp.where(w > 0, x, zero) for x in back]
                total = {c: here[c] + back[c] for c in (0, 2, 3, 4, 5)}
                delta = {c: here[c] - back[c] for c in (1, 3, 5)}
                level = []
                for i in range(3):
                    x = total[SLOT[i][0]]
                    m, q = delta[SLOT[i][1]], total[SLOT[i][2]]
                    level.append((x, m + q, m - q))
            for i in range(3):
                if t < layers:
                    x, y, z = level[i]
                    plus, minus = x + y, x + z
                    if t > 0:
                        plus, minus = plus + lower[i][0], minus + lower[i][1]
                else:
                    plus, minus = lower[i]
                part[i, t, w] = scale * (plus + before(minus, masks))
            if t < layers:
                lower = [(y - x, z - x) for x, y, z in level]
        return carry

    lax.fori_loop(0, columns + 1, column, 0)

    top = columns - 1
    for i in range(3):
        for t in range(layers + 1):
            for k in range(2):
                low, high = part[i, t, k], part[i, t, top + k]
                sa[i, t, k] = jnp.where(w_even, high, low)
                sb[i, t, k] = jnp.where(w_even, low, high)
    for c in range(6):
        for t in range(layers):
            for w in range(columns):
                new[c, t, pl.ds(w, sub, stride=columns), :] = tau[c, t, w]


def join_kernel(dims, ends, part, wa, wb, full, sa, sb):
    layers, columns, sub = dims
    w_at, t_at, w_even, t_even = place()
    zero = jnp.zeros((sub, LANES), jnp.float32)
    w_low, w_high = w_at > 0, w_at < ends[0] - 1
    for i in range(3):
        for t in range(layers + 1):
            low = [jnp.where(w_low, jnp.where(w_even, wb[i, t, k], wa[i, t, k]), zero) for k in range(2)]
            high = [jnp.where(w_high, jnp.where(w_even, wa[i, t, k], wb[i, t, k]), zero) for k in range(2)]
            full[i, t, 0] = low[0]
            full[i, t, 1] = part[i, t, 0] + low[1]
            for w in range(1, columns):
                full[i, t, w + 1] = part[i, t, w]
            full[i, t, columns + 1] = jnp.where(w_high, part[i, t, columns] + high[0], zero)
            full[i, t, columns + 2] = high[1]
    for i in range(3):
        for w in range(columns + 3):
            for k in range(2):
                low, high = full[i, k, w], full[i, layers - 1 + k, w]
                sa[i, k, w] = jnp.where(t_even, high, low)
                sb[i, k, w] = jnp.where(t_even, low, high)


def krylov_kernel(dims, ends, full, ta, tb, stiff, wsa, wsb, tsa, tsb, force, image, sums, ext, img):
    layers, columns, sub = dims
    w_at, t_at, w_even, t_even = place()
    masks = edge_masks(sub)
    zero = jnp.zeros((sub, LANES), jnp.float32)
    w_high = w_at < ends[0] - 1
    t_low, t_high = t_at > 0, t_at < ends[1] - 1
    for i in range(3):
        for w in range(columns + 3):
            low = [jnp.where(t_low, jnp.where(t_even, tb[i, k, w], ta[i, k, w]), zero) for k in range(2)]
            high = [jnp.where(t_high, jnp.where(t_even, ta[i, k, w], tb[i, k, w]), zero) for k in range(2)]
            ext[i, 0, w] = low[0]
            ext[i, 1, w] = full[i, 0, w] + low[1]
            for t in range(1, layers):
                ext[i, t + 1, w] = full[i, t, w]
            ext[i, layers + 1, w] = jnp.where(t_high, full[i, layers, w] + high[0], zero)
            ext[i, layers + 2, w] = high[1]

    def apply(i, t, w, diagonal):
        here = ext[i, t + 1, w + 1]
        beside = ext[i, t, w + 1] + ext[i, t + 2, w + 1]
        beside = beside + (ext[i, t + 1, w] + ext[i, t + 1, w + 2])
        beside = beside + (before(here, masks) + after(here, masks))
        return here, diagonal * here - beside

    for t in range(layers):
        d = 6.0 + jnp.where(w_even, wsa[t], wsb[t])
        for i in range(3):
            _, g = apply(i, t, columns, d)
            img[i, t, columns] = jnp.where(w_high, g, zero)
    for w in range(columns):
        d = 6.0 + jnp.where(
            t_even, row_of(tsa, (), w, columns, sub), row_of(tsb, (), w, columns, sub)
        )
        for i in range(3):
            _, g = apply(i, layers, w, d)
            img[i, layers, w] = jnp.where(t_high, g, zero)
    for t in range(layers):
        for w in range(columns):
            d = 6.0 + row_of(stiff, (t,), w, columns, sub)
            for i in range(3):
                f, g = apply(i, t, w, d)
                img[i, t, w] = g
                image[i, t, w] = g
                force[i, t, w] = f
    m0 = m1 = m2 = m3 = me = zero
    for t in range(layers):
        for w in range(columns):
            d = 6.0 + row_of(stiff, (t,), w, columns, sub)
            square = zero
            for i in range(3):
                f, g = ext[i, t + 1, w + 1], img[i, t, w]
                m0, m1 = m0 + f * f, m1 + f * g
                square = square + g * g
                me = me + g * (img[i, t + 1, w] + img[i, t, w + 1] + after(g, masks))
            m2, m3 = m2 + square, m3 + d * square
    m3 = m3 - 2.0 * me
    lane = lax.broadcasted_iota(jnp.int32, (1, LANES), 1)
    line = jnp.zeros((1, LANES), jnp.float32)
    for k, m in enumerate((m0, m1, m2, m3)):
        line = jnp.where(lane == k, jnp.sum(m, keepdims=True), line)
    sums[...] = jnp.broadcast_to(line[None], sums.shape)


def finish_kernel(dims, sums, force, image, out):
    layers, columns, sub = dims
    line = jnp.sum(sums[...], axis=0)
    lane = lax.broadcasted_iota(jnp.int32, (1, LANES), 1)
    m0, m1, m2, m3 = [
        jnp.sum(jnp.where(lane == k, line, 0.0), axis=1, keepdims=True) for k in range(4)
    ]
    a1 = m0 / m1
    left = a1 * a1 * m2 - m0
    grow = 1.0 + left / m0
    a2 = left / (grow * grow * m1 - 2.0 * grow * a1 * m2 + a1 * a1 * m3)
    c0 = jnp.broadcast_to(a1 + a2 * grow, (sub, LANES))
    c1 = jnp.broadcast_to(a1 * a2, (sub, LANES))
    for i in range(3):
        for t in range(layers):
            for w in range(columns):
                out[i, t, pl.ds(w, sub, stride=columns), :] = (
                    c0 * force[i, t, w] - c1 * image[i, t, w]
                )


def call(kernel, shapes, scratch=()):
    return pl.pallas_call(
        kernel,
        out_shape=[jax.ShapeDtypeStruct(s, jnp.float32) for s in shapes],
        scratch_shapes=[pltpu.VMEM(s, jnp.float32) for s in scratch],
        compiler_params=pltpu.CompilerParams(vmem_limit_bytes=VMEM_LIMIT),
    )


def on_device(ends, deviation, velocity, stiffness):
    _, layers, columns, length = deviation.shape
    sub = length // LANES
    dims = (layers, columns, sub)
    rows = columns * sub
    tile = (sub, LANES)
    w_first, w_second, t_first, t_second = swap_pairs(*ends)
    dev, vel, stiff = as_tiles(deviation), as_tiles(velocity), as_tiles(stiffness)

    wa, wb, ta, tb = call(
        functools.partial(pack_kernel, dims),
        [(10, layers, *tile)] * 2 + [(10, rows, LANES)] * 2,
    )(dev, vel, stiff)
    wa, wb = swap(wa, w_first), swap(wb, w_second)
    ta, tb = swap(ta, t_first), swap(tb, t_second)

    new, part, sa, sb = call(
        functools.partial(advance_kernel, dims, ends),
        [(6, layers, rows, LANES), (3, layers + 1, columns + 1, *tile)]
        + [(3, layers + 1, 2, *tile)] * 2,
        [(9, layers + 2, columns + 2, *tile), (6, layers, columns, *tile)],
    )(dev, vel, wa, wb, ta, tb)
    sa, sb = swap(sa, w_first), swap(sb, w_second)

    full, sa, sb = call(
        functools.partial(join_kernel, dims, ends),
        [(3, layers + 1, columns + 3, *tile)] + [(3, 2, columns + 3, *tile)] * 2,
    )(part, sa, sb)
    sa, sb = swap(sa, t_first), swap(sb, t_second)

    force, image, sums = call(
        functools.partial(krylov_kernel, dims, ends),
        [(3, layers, columns, *tile)] * 2 + [(ends[0] * ends[1], 1, LANES)],
        [(3, layers + 3, columns + 3, *tile), (3, layers + 1, columns + 1, *tile)],
    )(full, sa, sb, stiff, wa[9], wb[9], ta[9], tb[9])
    sums = lax.all_to_all(sums, AXES, 0, 0, tiled=True)

    (out,) = call(functools.partial(finish_kernel, dims), [(3, layers, rows, LANES)])(
        sums, force, image
    )
    return from_tiles(new, columns), from_tiles(out, columns)


def solution(mesh):
    placed = (
        P(None, "thick", "width", None),
        P(None, "thick", "width", None),
        P("thick", "width", None),
    )
    ends = (mesh.shape["width"], mesh.shape["thick"])
    return jax.shard_map(
        functools.partial(on_device, ends),
        mesh=mesh,
        in_specs=placed,
        out_specs=(P(None, "thick", "width", None), P(None, "thick", "width", None)),
        check_vma=False,
    )
```

```python
import functools

import jax
import jax.numpy as jnp
from jax import lax
from jax.experimental import pallas as pl
from jax.experimental.pallas import tpu as pltpu
from jax.sharding import PartitionSpec as P

TIME_STEP = 0.1
RELAX_TIME = 1.0
MOBILITY = 0.3
MODULUS = 10.0
LANES = 128
AXES = ("width", "thick")
PAIRS = ((0, 0), (1, 1), (2, 2), (0, 1), (0, 2), (1, 2))
SLOT = ((0, 3, 4), (3, 1, 5), (4, 5, 2))
VMEM_LIMIT = 40 * 1024 * 1024
PACK_LIMIT = 53 * 1024 * 1024


def swap_pairs(wide, thick):
    def flat(fn):
        return [
            (w * thick + t, fn(w, t)[0] * thick + fn(w, t)[1])
            for w in range(wide)
            for t in range(thick)
        ]

    def width_second(w, t):
        return (w, t ^ 1) if w in (0, wide - 1) else (((w - 1) ^ 1) + 1, t)

    def thick_second(w, t):
        return (w, thick - 1 - t) if t in (0, thick - 1) else (w, ((t - 1) ^ 1) + 1)

    return (
        flat(lambda w, t: (w ^ 1, t)),
        flat(width_second),
        flat(lambda w, t: (w, t ^ 1)),
        flat(thick_second),
    )


def swap(value, pairs):
    return lax.ppermute(value, AXES, pairs)


def as_tiles(x):
    *lead, w, length = x.shape
    x = x.reshape(*lead, w, length // LANES, LANES)
    return jnp.swapaxes(x, -3, -2).reshape(*lead, length // LANES * w, LANES)


def from_tiles(x, w):
    *lead, rows, lanes = x.shape
    x = x.reshape(*lead, rows // w, w, lanes)
    return jnp.swapaxes(x, -3, -2).reshape(*lead, w, rows // w * lanes)


def row_of(ref, lead, w, columns, sub):
    return ref[(*lead, pl.ds(w, sub, stride=columns), slice(None))]


def edge_masks(sub):
    lane = lax.broadcasted_iota(jnp.int32, (sub, LANES), 1)
    row = lax.broadcasted_iota(jnp.int32, (sub, LANES), 0)
    first, last = lane == 0, lane == LANES - 1
    return first, first & (row == 0), last, last & (row == sub - 1)


def before(x, masks):
    first, corner = masks[0], masks[1]
    near = pltpu.roll(x, 1, axis=1)
    far = pltpu.roll(near, 1, axis=0)
    return jnp.where(corner, 0.0, jnp.where(first, far, near))


def after(x, masks):
    last, corner = masks[2], masks[3]
    sub = x.shape[0]
    near = pltpu.roll(x, LANES - 1, axis=1)
    far = pltpu.roll(near, sub - 1, axis=0)
    return jnp.where(corner, 0.0, jnp.where(last, far, near))


def halves(axis, end):
    at = lax.axis_index(axis)
    even = at % 2 == 0
    has_low, has_high = at > 0, at < end - 1

    def low(first, second):
        return jnp.where(has_low, jnp.where(even, second, first), 0.0)

    def high(first, second):
        return jnp.where(has_high, jnp.where(even, first, second), 0.0)

    def send(low_face, high_face):
        return jnp.where(even, high_face, low_face), jnp.where(even, low_face, high_face)

    return low, high, send, has_high


def fetch(sources, targets, sems):
    copies = []
    for source, target in zip(sources, targets):
        for c in range(source.shape[0]):
            copies.append(pltpu.make_async_copy(source.at[c], target.at[c], sems.at[len(copies)]))
    for copy in copies:
        copy.start()
    for copy in copies:
        copy.wait()


def pack_kernel(dims, ends, dev_hbm, vel_hbm, wa, wb, ta, tb, dev, vel, sems):
    layers, columns, sub = dims
    send_w = halves("width", ends[0])[2]
    send_t = halves("thick", ends[1])[2]
    fetch((dev_hbm, vel_hbm), (dev, vel), sems)
    for c in range(9):
        ref, lead = (dev, (c,)) if c < 6 else (vel, (c - 6,))
        for t in range(layers):
            low = row_of(ref, (*lead, t), 0, columns, sub)
            high = row_of(ref, (*lead, t), columns - 1, columns, sub)
            wa[c, t], wb[c, t] = send_w(low, high)
        ta[c], tb[c] = send_t(ref[(*lead, 0)], ref[(*lead, layers - 1)])


HALF = 0.5 * TIME_STEP


def inner_kernel(dims, dev, vel, after_pack, ext, tau):
    layers, columns, sub = dims
    masks = edge_masks(sub)
    zero = jnp.zeros((sub, LANES), jnp.float32)
    for c in range(9):
        ref, lead = (dev, (c,)) if c < 6 else (vel, (c - 6,))
        for t in range(layers):
            for w in range(columns):
                ext[c, t + 1, w + 1] = row_of(ref, (*lead, t), w, columns, sub)
            ext[c, t + 1, 0] = zero
            ext[c, t + 1, columns + 1] = zero
        for w in range(columns):
            ext[c, 0, w + 1] = zero
            ext[c, layers + 1, w + 1] = zero

    def cell(t, w):
        def at(c, d, off):
            where = [t + 1, w + 1]
            where[d] = where[d] + off
            return ext[c, where[0], where[1]]

        s = [ext[c, t + 1, w + 1] for c in range(6)]
        u = [ext[6 + c, t + 1, w + 1] for c in range(3)]
        grad = [
            [HALF * (at(6 + i, j, 1) - at(6 + i, j, -1)) for j in range(2)]
            + [HALF * (after(u[i], masks) - before(u[i], masks))]
            for i in range(3)
        ]
        pos = [TIME_STEP * jnp.maximum(u[d], 0.0) for d in range(3)]
        neg = [TIME_STEP * jnp.minimum(u[d], 0.0) for d in range(3)]
        keep = (1.0 - TIME_STEP / RELAX_TIME) - (
            (pos[0] - neg[0]) + (pos[1] - neg[1]) + (pos[2] - neg[2])
        )
        bend = HALF * MOBILITY / RELAX_TIME
        scaled = [bend * s[c] for c in range(6)]
        turn = [[grad[i][k] - scaled[SLOT[i][k]] for k in range(3)] for i in range(3)]
        for p, (i, j) in enumerate(PAIRS):
            out = keep * s[p]
            for d in range(2):
                out = out + pos[d] * at(p, d, -1) - neg[d] * at(p, d, 1)
            out = out + pos[2] * before(s[p], masks) - neg[2] * after(s[p], masks)
            if i == j:
                more = grad[i][i]
                for k in range(3):
                    more = more + turn[i][k] * s[SLOT[k][i]]
                out = out + 2.0 * more
            else:
                out = out + (grad[i][j] + grad[j][i])
                for k in range(3):
                    out = out + turn[i][k] * s[SLOT[k][j]] + turn[j][k] * s[SLOT[k][i]]
            tau[p, t, w] = out

    def cells(step, carry):
        t, w = step // (columns // 2), step % (columns // 2)
        cell(t, 2 * w)
        cell(t, 2 * w + 1)
        return carry

    lax.fori_loop(0, layers * columns // 2, cells, 0)


def nodes(dims, tau, columns_of_nodes, put):
    layers, columns, sub = dims
    masks = edge_masks(sub)
    scale = 0.25 * MODULUS
    for w in columns_of_nodes:
        lower = None
        for t in range(layers + 1):
            level = []
            if t < layers:
                here = [tau[c, t, w] for c in range(6)] if w < columns else None
                back = [tau[c, t, w - 1] for c in range(6)] if w > 0 else None
                if here is None:
                    total, delta = back, [-x for x in back]
                elif back is None:
                    total = delta = here
                else:
                    total = [a + b for a, b in zip(here, back)]
                    delta = [a - b for a, b in zip(here, back)]
                for i in range(3):
                    m, q = delta[SLOT[i][1]], total[SLOT[i][2]]
                    level.append((total[SLOT[i][0]], m + q, m - q))
            for i in range(3):
                if t < layers:
                    x, y, z = level[i]
                    plus, minus = x + y, x + z
                    if t > 0:
                        plus, minus = plus + lower[i][0], minus + lower[i][1]
                else:
                    plus, minus = lower[i]
                put(i, t, w, scale * (plus + before(minus, masks)))
            lower = [(y - x, z - x) for x, y, z in level]


def outer_kernel(dims, ends, tau_in, ext, wa, wb, ta, tb, stiff, tau, part, sa, sb):
    layers, columns, sub = dims
    w_low, w_high, send_w, _ = halves("width", ends[0])
    t_low, t_high, _, _ = halves("thick", ends[1])

    def correct(t, w, d, sign, halo):
        s = [ext[c, t + 1, w + 1] for c in range(6)]
        u = ext[6 + d, t + 1, w + 1]
        speed = jnp.maximum(u, 0.0) if sign < 0 else -jnp.minimum(u, 0.0)
        speed = TIME_STEP * speed
        h = [(sign * HALF) * halo[6 + i] for i in range(3)]
        q = [s[SLOT[d][j]] for j in range(3)]
        q[d] = q[d] + 1.0
        for p, (i, j) in enumerate(PAIRS):
            bent = 2.0 * (h[i] * q[i]) if i == j else h[i] * q[j] + h[j] * q[i]
            tau[p, t, w] = tau[p, t, w] + (speed * halo[p] + bent)

    def side(t, carry):
        a, b = [wa[c, t] for c in range(9)], [wb[c, t] for c in range(9)]
        correct(t, 0, 1, -1.0, [w_low(x, y) for x, y in zip(a, b)])
        correct(t, columns - 1, 1, 1.0, [w_high(x, y) for x, y in zip(a, b)])
        return carry

    lax.fori_loop(0, layers, side, 0)
    for w in range(columns):
        a = [row_of(ta, (c,), w, columns, sub) for c in range(9)]
        b = [row_of(tb, (c,), w, columns, sub) for c in range(9)]
        correct(0, w, 0, -1.0, [t_low(x, y) for x, y in zip(a, b)])
        correct(layers - 1, w, 0, 1.0, [t_high(x, y) for x, y in zip(a, b)])

    slot = {0: 0, 1: 1, columns - 1: 2, columns: 3}

    def put(i, t, w, value):
        part[i, t, slot[w]] = value

    nodes(dims, tau, slot, put)
    count = 2 * (layers + 1)
    for i in range(3):
        for t in range(layers + 1):
            for k in range(2):
                at = i * count + t * 2 + k
                sa[at], sb[at] = send_w(part[i, t, k], part[i, t, 2 + k])
    for t in range(layers):
        row = row_of(stiff, (t,), 0, columns, sub)
        sa[3 * count + t] = row
        sb[3 * count + t] = row


def middle_kernel(dims, ends, tau, part, stiff, mid, sa, sb):
    layers, columns, sub = dims
    send_t = halves("thick", ends[1])[2]

    def put(i, t, w, value):
        mid[i, t, w - 1] = value

    nodes(dims, tau, range(2, columns - 1), put)
    for i in range(3):
        for t in range(layers + 1):
            mid[i, t, 0] = part[i, t, 1]
            mid[i, t, columns - 2] = part[i, t, 2]
    inner = columns - 1
    for i in range(3):
        for k in range(2):
            for w in range(inner):
                at = (i * 2 + k) * inner + w
                sa[at], sb[at] = send_t(mid[i, k, w], mid[i, layers - 1 + k, w])
    for w in range(columns):
        row = row_of(stiff, (0,), w, columns, sub)
        sa[6 * inner + w] = row
        sb[6 * inner + w] = row


def emit_kernel(dims, tau, after_join, new):
    layers, columns, sub = dims
    for c in range(6):
        for t in range(layers):
            for w in range(columns):
                new[c, t, pl.ds(w, sub, stride=columns), :] = tau[c, t, w]


def join_kernel(dims, ends, part, wa, wb, side, sa, sb):
    layers, columns, sub = dims
    w_low, w_high, _, has_high = halves("width", ends[0])
    send_t = halves("thick", ends[1])[2]
    count = 2 * (layers + 1)
    for i in range(3):
        for t in range(layers + 1):
            at = i * count + t * 2
            below = [w_low(wa[at + k], wb[at + k]) for k in range(2)]
            above = [w_high(wa[at + k], wb[at + k]) for k in range(2)]
            side[i, t, 0] = below[0]
            side[i, t, 1] = part[i, t, 0] + below[1]
            side[i, t, 2] = jnp.where(has_high, part[i, t, 3] + above[0], 0.0)
            side[i, t, 3] = above[1]
    for i in range(3):
        for k in range(2):
            for w in range(4):
                at = (i * 2 + k) * 4 + w
                sa[at], sb[at] = send_t(side[i, k, w], side[i, layers - 1 + k, w])


def krylov_kernel(
    dims, ends, mid, side, ma, mb, ja, jb, wa, wb, stiff, force, image, sums, ext, img
):
    layers, columns, sub = dims
    w_high = halves("width", ends[0])[1]
    has_right = halves("width", ends[0])[3]
    t_low, t_high, _, has_top = halves("thick", ends[1])
    masks = edge_masks(sub)
    zero = jnp.zeros((sub, LANES), jnp.float32)
    inner = columns - 1
    edge = {0: 0, 1: 1, columns + 1: 2, columns + 2: 3}
    for i in range(3):
        for w in range(columns + 3):
            if w in edge:
                own, a, b, at, step = side, ja, jb, edge[w], 4
            else:
                own, a, b, at, step = mid, ma, mb, w - 2, inner
            a = [a[(i * 2 + k) * step + at] for k in range(2)]
            b = [b[(i * 2 + k) * step + at] for k in range(2)]
            below = [t_low(x, y) for x, y in zip(a, b)]
            above = [t_high(x, y) for x, y in zip(a, b)]
            ext[i, 0, w] = below[0]
            ext[i, 1, w] = own[i, 0, at] + below[1]
            for t in range(1, layers):
                ext[i, t + 1, w] = own[i, t, at]
            ext[i, layers + 1, w] = jnp.where(has_top, own[i, layers, at] + above[0], 0.0)
            ext[i, layers + 2, w] = above[1]

    def apply(i, t, w, diagonal):
        here = ext[i, t + 1, w + 1]
        beside = ext[i, t, w + 1] + ext[i, t + 2, w + 1]
        beside = beside + (ext[i, t + 1, w] + ext[i, t + 1, w + 2])
        beside = beside + (before(here, masks) + after(here, masks))
        return here, diagonal * here - beside

    count = 2 * (layers + 1)
    for t in range(layers):
        d = 6.0 + w_high(wa[3 * count + t], wb[3 * count + t])
        for i in range(3):
            _, g = apply(i, t, columns, d)
            img[i, t, columns] = jnp.where(has_right, g, 0.0)
    for w in range(columns):
        d = 6.0 + t_high(ma[6 * inner + w], mb[6 * inner + w])
        for i in range(3):
            _, g = apply(i, layers, w, d)
            img[i, layers, w] = jnp.where(has_top, g, 0.0)
    for t in range(layers):
        for w in range(columns):
            d = 6.0 + row_of(stiff, (t,), w, columns, sub)
            for i in range(3):
                f, g = apply(i, t, w, d)
                img[i, t, w] = g
                image[i, t, w] = g
                force[i, t, w] = f
    m0 = m1 = m2 = m3 = me = zero
    for t in range(layers):
        for w in range(columns):
            d = 6.0 + row_of(stiff, (t,), w, columns, sub)
            square = zero
            for i in range(3):
                f, g = ext[i, t + 1, w + 1], img[i, t, w]
                m0, m1 = m0 + f * f, m1 + f * g
                square = square + g * g
                me = me + g * (img[i, t + 1, w] + img[i, t, w + 1] + after(g, masks))
            m2, m3 = m2 + square, m3 + d * square
    m3 = m3 - 2.0 * me
    lane = lax.broadcasted_iota(jnp.int32, (1, LANES), 1)
    line = jnp.zeros((1, LANES), jnp.float32)
    for k, m in enumerate((m0, m1, m2, m3)):
        line = jnp.where(lane == k, jnp.sum(m, keepdims=True), line)
    sums[...] = jnp.broadcast_to(line[None], sums.shape)


def finish_kernel(dims, sums, force, image, out):
    layers, columns, sub = dims
    line = jnp.sum(sums[...], axis=0)
    lane = lax.broadcasted_iota(jnp.int32, (1, LANES), 1)
    m0, m1, m2, m3 = [
        jnp.sum(jnp.where(lane == k, line, 0.0), axis=1, keepdims=True) for k in range(4)
    ]
    a1 = m0 / m1
    left = a1 * a1 * m2 - m0
    grow = 1.0 + left / m0
    a2 = left / (grow * grow * m1 - 2.0 * grow * a1 * m2 + a1 * a1 * m3)
    c0 = jnp.broadcast_to(a1 + a2 * grow, (sub, LANES))
    c1 = jnp.broadcast_to(a1 * a2, (sub, LANES))
    for i in range(3):
        for t in range(layers):
            for w in range(columns):
                out[i, t, pl.ds(w, sub, stride=columns), :] = (
                    c0 * force[i, t, w] - c1 * image[i, t, w]
                )


def call(
    kernel, shapes, scratch=(), hbm=(), count=0, copies=0, aliases=None, cost=None, limit=VMEM_LIMIT
):
    anywhere, local = pl.BlockSpec(memory_space=pltpu.HBM), pl.BlockSpec(memory_space=pltpu.VMEM)
    extra = [pltpu.SemaphoreType.DMA((copies,))] if copies else []
    more = {}
    if cost is not None:
        more["cost_estimate"] = pl.CostEstimate(flops=0, transcendentals=0, bytes_accessed=cost)
    return pl.pallas_call(
        kernel,
        out_shape=[jax.ShapeDtypeStruct(s, jnp.float32) for s in shapes],
        in_specs=[anywhere if k in hbm else local for k in range(count)],
        scratch_shapes=[pltpu.VMEM(s, jnp.float32) for s in scratch] + extra,
        input_output_aliases=aliases or {},
        compiler_params=pltpu.CompilerParams(vmem_limit_bytes=limit),
        **more,
    )


def on_device(ends, deviation, velocity, stiffness):
    _, layers, columns, length = deviation.shape
    sub = length // LANES
    dims = (layers, columns, sub)
    rows = columns * sub
    tile = (sub, LANES)
    w_first, w_second, t_first, t_second = swap_pairs(*ends)
    dev, vel, stiff = as_tiles(deviation), as_tiles(velocity), as_tiles(stiffness)

    wa, wb, ta, tb = call(
        functools.partial(pack_kernel, dims, ends),
        [(9, layers, *tile)] * 2 + [(9, rows, LANES)] * 2,
        [(6, layers, rows, LANES), (3, layers, rows, LANES)],
        hbm=(0, 1), count=2, copies=9, limit=PACK_LIMIT,
    )(dev, vel)
    packed = wa
    tb = swap(tb, t_second)
    wb = swap(wb, w_second)
    wa = swap(wa, w_first)
    ta = swap(ta, t_first)

    ext, tau = call(
        functools.partial(inner_kernel, dims),
        [(9, layers + 2, columns + 2, *tile), (6, layers, columns, *tile)],
        hbm=(2,), count=3, cost=12 * 1024 * 1024,
    )(dev, vel, packed)

    face = 6 * (layers + 1) + layers
    tau, part, sa, sb = call(
        functools.partial(outer_kernel, dims, ends),
        [(6, layers, columns, *tile), (3, layers + 1, 4, *tile)] + [(face, *tile)] * 2,
        count=7, aliases={0: 0},
    )(tau, ext, wa, wb, ta, tb, stiff)
    wb = swap(sb, w_second)
    wa = swap(sa, w_first)

    broad = 6 * (columns - 1) + columns
    mid, sa, sb = call(
        functools.partial(middle_kernel, dims, ends),
        [(3, layers + 1, columns - 1, *tile)] + [(broad, *tile)] * 2,
        count=3, cost=2 * 1024 * 1024,
    )(tau, part, stiff)
    mb = swap(sb, t_second)
    ma = swap(sa, t_first)

    side, sa, sb = call(
        functools.partial(join_kernel, dims, ends),
        [(3, layers + 1, 4, *tile)] + [(24, *tile)] * 2,
        count=3,
    )(part, wa, wb)
    jb = swap(sb, t_second)
    ja = swap(sa, t_first)

    (new,) = call(
        functools.partial(emit_kernel, dims), [(6, layers, rows, LANES)],
        hbm=(1,), count=2, cost=6 * 1024 * 1024,
    )(tau, side)

    force, image, sums = call(
        functools.partial(krylov_kernel, dims, ends),
        [(3, layers, columns, *tile)] * 2 + [(ends[0] * ends[1], 1, LANES)],
        [(3, layers + 3, columns + 3, *tile), (3, layers + 1, columns + 1, *tile)],
        count=9,
    )(mid, side, ma, mb, ja, jb, wa, wb, stiff)
    sums = lax.all_to_all(sums, AXES, 0, 0, tiled=True)

    (out,) = call(
        functools.partial(finish_kernel, dims), [(3, layers, rows, LANES)], count=3
    )(sums, force, image)
    return from_tiles(new, columns), from_tiles(out, columns)


def solution(mesh):
    placed = (
        P(None, "thick", "width", None),
        P(None, "thick", "width", None),
        P("thick", "width", None),
    )
    ends = (mesh.shape["width"], mesh.shape["thick"])
    return jax.shard_map(
        functools.partial(on_device, ends),
        mesh=mesh,
        in_specs=placed,
        out_specs=(P(None, "thick", "width", None), P(None, "thick", "width", None)),
        check_vma=False,
    )
```

```python
import functools

import jax
import jax.numpy as jnp
from jax import lax
from jax.experimental import pallas as pl
from jax.experimental.pallas import tpu as pltpu
from jax.sharding import PartitionSpec as P

TIME_STEP = 0.1
RELAX_TIME = 1.0
MOBILITY = 0.3
MODULUS = 10.0
LANES = 128
AXES = ("width", "thick")
PAIRS = ((0, 0), (1, 1), (2, 2), (0, 1), (0, 2), (1, 2))
SLOT = ((0, 3, 4), (3, 1, 5), (4, 5, 2))
VMEM_LIMIT = 40 * 1024 * 1024
PACK_LIMIT = 53 * 1024 * 1024


def swap_pairs(wide, thick):
    def flat(fn):
        return [
            (w * thick + t, fn(w, t)[0] * thick + fn(w, t)[1])
            for w in range(wide)
            for t in range(thick)
        ]

    def width_second(w, t):
        return (w, t ^ 1) if w in (0, wide - 1) else (((w - 1) ^ 1) + 1, t)

    def thick_second(w, t):
        return (w, thick - 1 - t) if t in (0, thick - 1) else (w, ((t - 1) ^ 1) + 1)

    return (
        flat(lambda w, t: (w ^ 1, t)),
        flat(width_second),
        flat(lambda w, t: (w, t ^ 1)),
        flat(thick_second),
    )


def swap(value, pairs):
    return lax.ppermute(value, AXES, pairs)


def as_tiles(x):
    *lead, w, length = x.shape
    x = x.reshape(*lead, w, length // LANES, LANES)
    return jnp.swapaxes(x, -3, -2).reshape(*lead, length // LANES * w, LANES)


def from_tiles(x, w):
    *lead, rows, lanes = x.shape
    x = x.reshape(*lead, rows // w, w, lanes)
    return jnp.swapaxes(x, -3, -2).reshape(*lead, w, rows // w * lanes)


def row_of(ref, lead, w, columns, sub):
    return ref[(*lead, pl.ds(w, sub, stride=columns), slice(None))]


def edge_masks(sub):
    lane = lax.broadcasted_iota(jnp.int32, (sub, LANES), 1)
    row = lax.broadcasted_iota(jnp.int32, (sub, LANES), 0)
    first, last = lane == 0, lane == LANES - 1
    return first, first & (row == 0), last, last & (row == sub - 1)


def before(x, masks):
    first, corner = masks[0], masks[1]
    near = pltpu.roll(x, 1, axis=1)
    far = pltpu.roll(near, 1, axis=0)
    return jnp.where(corner, 0.0, jnp.where(first, far, near))


def after(x, masks):
    last, corner = masks[2], masks[3]
    sub = x.shape[0]
    near = pltpu.roll(x, LANES - 1, axis=1)
    far = pltpu.roll(near, sub - 1, axis=0)
    return jnp.where(corner, 0.0, jnp.where(last, far, near))


def halves(axis, end):
    at = lax.axis_index(axis)
    even = at % 2 == 0
    has_low, has_high = at > 0, at < end - 1

    def low(first, second):
        return jnp.where(has_low, jnp.where(even, second, first), 0.0)

    def high(first, second):
        return jnp.where(has_high, jnp.where(even, first, second), 0.0)

    def send(low_face, high_face):
        return jnp.where(even, high_face, low_face), jnp.where(even, low_face, high_face)

    return low, high, send, has_high


def fetch(sources, targets, sems):
    copies = []
    for source, target in zip(sources, targets):
        for c in range(source.shape[0]):
            copies.append(pltpu.make_async_copy(source.at[c], target.at[c], sems.at[len(copies)]))
    for copy in copies:
        copy.start()
    for copy in copies:
        copy.wait()


def pack_kernel(dims, ends, dev_hbm, vel_hbm, wa, wb, ta, tb, dev, vel, sems):
    layers, columns, sub = dims
    send_w = halves("width", ends[0])[2]
    send_t = halves("thick", ends[1])[2]
    fetch((dev_hbm, vel_hbm), (dev, vel), sems)
    for c in range(9):
        ref, lead = (dev, (c,)) if c < 6 else (vel, (c - 6,))
        for t in range(layers):
            low = row_of(ref, (*lead, t), 0, columns, sub)
            high = row_of(ref, (*lead, t), columns - 1, columns, sub)
            wa[c, t], wb[c, t] = send_w(low, high)
        ta[c], tb[c] = send_t(ref[(*lead, 0)], ref[(*lead, layers - 1)])


HALF = 0.5 * TIME_STEP


def inner_kernel(dims, dev, vel, after_pack, stiff, ext, tau):
    layers, columns, sub = dims
    masks = edge_masks(sub)
    zero = jnp.zeros((sub, LANES), jnp.float32)
    for c in range(9):
        ref, lead = (dev, (c,)) if c < 6 else (vel, (c - 6,))
        for t in range(layers):
            for w in range(columns):
                ext[c, t + 1, w + 1] = row_of(ref, (*lead, t), w, columns, sub)
            ext[c, t + 1, 0] = zero
            ext[c, t + 1, columns + 1] = zero
        for w in range(columns):
            ext[c, 0, w + 1] = zero
            ext[c, layers + 1, w + 1] = zero

    def cell(t, w):
        def at(c, d, off):
            where = [t + 1, w + 1]
            where[d] = where[d] + off
            return ext[c, where[0], where[1]]

        s = [ext[c, t + 1, w + 1] for c in range(6)]
        u = [ext[6 + c, t + 1, w + 1] for c in range(3)]
        grad = [
            [HALF * (at(6 + i, j, 1) - at(6 + i, j, -1)) for j in range(2)]
            + [HALF * (after(u[i], masks) - before(u[i], masks))]
            for i in range(3)
        ]
        pos = [TIME_STEP * jnp.maximum(u[d], 0.0) for d in range(3)]
        neg = [TIME_STEP * jnp.minimum(u[d], 0.0) for d in range(3)]
        keep = (1.0 - TIME_STEP / RELAX_TIME) - (
            (pos[0] - neg[0]) + (pos[1] - neg[1]) + (pos[2] - neg[2])
        )
        bend = HALF * MOBILITY / RELAX_TIME
        scaled = [bend * s[c] for c in range(6)]
        turn = [[grad[i][k] - scaled[SLOT[i][k]] for k in range(3)] for i in range(3)]
        for p, (i, j) in enumerate(PAIRS):
            out = keep * s[p]
            for d in range(2):
                out = out + pos[d] * at(p, d, -1) - neg[d] * at(p, d, 1)
            out = out + pos[2] * before(s[p], masks) - neg[2] * after(s[p], masks)
            if i == j:
                more = grad[i][i]
                for k in range(3):
                    more = more + turn[i][k] * s[SLOT[k][i]]
                out = out + 2.0 * more
            else:
                out = out + (grad[i][j] + grad[j][i])
                for k in range(3):
                    out = out + turn[i][k] * s[SLOT[k][j]] + turn[j][k] * s[SLOT[k][i]]
            tau[p, t, w] = out

    def cells(step, carry):
        t, w = step // (columns // 2), step % (columns // 2)
        cell(t, 2 * w)
        cell(t, 2 * w + 1)
        return carry

    lax.fori_loop(0, layers * columns // 2, cells, 0)


def nodes(dims, tau, columns_of_nodes, put):
    layers, columns, sub = dims
    masks = edge_masks(sub)
    scale = 0.25 * MODULUS
    for w in columns_of_nodes:
        lower = None
        for t in range(layers + 1):
            level = []
            if t < layers:
                here = [tau[c, t, w] for c in range(6)] if w < columns else None
                back = [tau[c, t, w - 1] for c in range(6)] if w > 0 else None
                if here is None:
                    total, delta = back, [-x for x in back]
                elif back is None:
                    total = delta = here
                else:
                    total = [a + b for a, b in zip(here, back)]
                    delta = [a - b for a, b in zip(here, back)]
                for i in range(3):
                    m, q = delta[SLOT[i][1]], total[SLOT[i][2]]
                    level.append((total[SLOT[i][0]], m + q, m - q))
            for i in range(3):
                if t < layers:
                    x, y, z = level[i]
                    plus, minus = x + y, x + z
                    if t > 0:
                        plus, minus = plus + lower[i][0], minus + lower[i][1]
                else:
                    plus, minus = lower[i]
                put(i, t, w, scale * (plus + before(minus, masks)))
            lower = [(y - x, z - x) for x, y, z in level]


def correct(tau, ext, t, w, d, sign, halo):
    s = [ext[c, t + 1, w + 1] for c in range(6)]
    u = ext[6 + d, t + 1, w + 1]
    speed = TIME_STEP * (jnp.maximum(u, 0.0) if sign < 0 else -jnp.minimum(u, 0.0))
    h = [(sign * HALF) * halo[6 + i] for i in range(3)]
    q = [s[SLOT[d][j]] for j in range(3)]
    q[d] = q[d] + 1.0
    for p, (i, j) in enumerate(PAIRS):
        bent = 2.0 * (h[i] * q[i]) if i == j else h[i] * q[j] + h[j] * q[i]
        tau[p, t, w] = tau[p, t, w] + (speed * halo[p] + bent)


def side_kernel(dims, ends, tau_in, ext, wa, wb, tau):
    layers, columns, sub = dims
    w_low, w_high, _, _ = halves("width", ends[0])

    def side(t, carry):
        a, b = [wa[c, t] for c in range(9)], [wb[c, t] for c in range(9)]
        correct(tau, ext, t, 0, 1, -1.0, [w_low(x, y) for x, y in zip(a, b)])
        correct(tau, ext, t, columns - 1, 1, 1.0, [w_high(x, y) for x, y in zip(a, b)])
        return carry

    lax.fori_loop(0, layers, side, 0)


def outer_kernel(dims, ends, tau_in, ext, ta, tb, stiff, tau, part, sa, sb):
    layers, columns, sub = dims
    send_w = halves("width", ends[0])[2]
    t_low, t_high, _, _ = halves("thick", ends[1])
    for w in range(columns):
        a = [row_of(ta, (c,), w, columns, sub) for c in range(9)]
        b = [row_of(tb, (c,), w, columns, sub) for c in range(9)]
        correct(tau, ext, 0, w, 0, -1.0, [t_low(x, y) for x, y in zip(a, b)])
        correct(tau, ext, layers - 1, w, 0, 1.0, [t_high(x, y) for x, y in zip(a, b)])

    slot = {0: 0, 1: 1, columns - 1: 2, columns: 3}

    def put(i, t, w, value):
        part[i, t, slot[w]] = value

    nodes(dims, tau, slot, put)
    count = 2 * (layers + 1)
    for i in range(3):
        for t in range(layers + 1):
            for k in range(2):
                at = i * count + t * 2 + k
                sa[at], sb[at] = send_w(part[i, t, k], part[i, t, 2 + k])
    for t in range(layers):
        row = row_of(stiff, (t,), 0, columns, sub)
        sa[3 * count + t] = row
        sb[3 * count + t] = row


def middle_kernel(dims, ends, tau, part, stiff, mid, sa, sb):
    layers, columns, sub = dims
    send_t = halves("thick", ends[1])[2]

    def put(i, t, w, value):
        mid[i, t, w - 1] = value

    nodes(dims, tau, range(2, columns - 1), put)
    for i in range(3):
        for t in range(layers + 1):
            mid[i, t, 0] = part[i, t, 1]
            mid[i, t, columns - 2] = part[i, t, 2]
    inner = columns - 1
    for i in range(3):
        for k in range(2):
            for w in range(inner):
                at = (i * 2 + k) * inner + w
                sa[at], sb[at] = send_t(mid[i, k, w], mid[i, layers - 1 + k, w])
    for w in range(columns):
        row = row_of(stiff, (0,), w, columns, sub)
        sa[6 * inner + w] = row
        sb[6 * inner + w] = row


def emit_kernel(dims, tau, after_join, new, done):
    layers, columns, sub = dims
    done[...] = jnp.zeros_like(done)
    for c in range(6):
        for t in range(layers):
            for w in range(columns):
                new[c, t, pl.ds(w, sub, stride=columns), :] = tau[c, t, w]


def join_kernel(dims, ends, part, wb, wa, side, sa, sb):
    layers, columns, sub = dims
    w_low, w_high, _, has_high = halves("width", ends[0])
    send_t = halves("thick", ends[1])[2]
    count = 2 * (layers + 1)
    for i in range(3):
        for t in range(layers + 1):
            at = i * count + t * 2
            below = [w_low(wa[at + k], wb[at + k]) for k in range(2)]
            above = [w_high(wa[at + k], wb[at + k]) for k in range(2)]
            side[i, t, 0] = below[0]
            side[i, t, 1] = part[i, t, 0] + below[1]
            side[i, t, 2] = jnp.where(has_high, part[i, t, 3] + above[0], 0.0)
            side[i, t, 3] = above[1]
    for i in range(3):
        for k in range(2):
            for w in range(4):
                at = (i * 2 + k) * 4 + w
                sa[at], sb[at] = send_t(side[i, k, w], side[i, layers - 1 + k, w])


def krylov_kernel(
    dims, ends, mid, side, mb, ma, jb, ja, wa, wb, stiff, after_emit, force, image, sums, ext, img
):
    layers, columns, sub = dims
    w_high = halves("width", ends[0])[1]
    has_right = halves("width", ends[0])[3]
    t_low, t_high, _, has_top = halves("thick", ends[1])
    masks = edge_masks(sub)
    zero = jnp.zeros((sub, LANES), jnp.float32)
    inner = columns - 1
    edge = {0: 0, 1: 1, columns + 1: 2, columns + 2: 3}
    for i in range(3):
        for w in range(columns + 3):
            if w in edge:
                own, a, b, at, step = side, ja, jb, edge[w], 4
            else:
                own, a, b, at, step = mid, ma, mb, w - 2, inner
            a = [a[(i * 2 + k) * step + at] for k in range(2)]
            b = [b[(i * 2 + k) * step + at] for k in range(2)]
            below = [t_low(x, y) for x, y in zip(a, b)]
            above = [t_high(x, y) for x, y in zip(a, b)]
            ext[i, 0, w] = below[0]
            ext[i, 1, w] = own[i, 0, at] + below[1]
            for t in range(1, layers):
                ext[i, t + 1, w] = own[i, t, at]
            ext[i, layers + 1, w] = jnp.where(has_top, own[i, layers, at] + above[0], 0.0)
            ext[i, layers + 2, w] = above[1]

    def apply(i, t, w, diagonal):
        here = ext[i, t + 1, w + 1]
        beside = ext[i, t, w + 1] + ext[i, t + 2, w + 1]
        beside = beside + (ext[i, t + 1, w] + ext[i, t + 1, w + 2])
        beside = beside + (before(here, masks) + after(here, masks))
        return here, diagonal * here - beside

    count = 2 * (layers + 1)
    for t in range(layers):
        d = 6.0 + w_high(wa[3 * count + t], wb[3 * count + t])
        for i in range(3):
            _, g = apply(i, t, columns, d)
            img[i, t, columns] = jnp.where(has_right, g, 0.0)
    for w in range(columns):
        d = 6.0 + t_high(ma[6 * inner + w], mb[6 * inner + w])
        for i in range(3):
            _, g = apply(i, layers, w, d)
            img[i, layers, w] = jnp.where(has_top, g, 0.0)
    for t in range(layers):
        for w in range(columns):
            d = 6.0 + row_of(stiff, (t,), w, columns, sub)
            for i in range(3):
                f, g = apply(i, t, w, d)
                img[i, t, w] = g
                image[i, t, w] = g
                force[i, t, w] = f
    m0 = m1 = m2 = m3 = me = zero
    for t in range(layers):
        for w in range(columns):
            d = 6.0 + row_of(stiff, (t,), w, columns, sub)
            square = zero
            for i in range(3):
                f, g = ext[i, t + 1, w + 1], img[i, t, w]
                m0, m1 = m0 + f * f, m1 + f * g
                square = square + g * g
                me = me + g * (img[i, t + 1, w] + img[i, t, w + 1] + after(g, masks))
            m2, m3 = m2 + square, m3 + d * square
    m3 = m3 - 2.0 * me
    lane = lax.broadcasted_iota(jnp.int32, (1, LANES), 1)
    line = jnp.zeros((1, LANES), jnp.float32)
    for k, m in enumerate((m0, m1, m2, m3)):
        line = jnp.where(lane == k, jnp.sum(m, keepdims=True), line)
    sums[...] = jnp.broadcast_to(line[None], sums.shape)


def finish_kernel(dims, sums, force, image, out):
    layers, columns, sub = dims
    line = jnp.sum(sums[...], axis=0)
    lane = lax.broadcasted_iota(jnp.int32, (1, LANES), 1)
    m0, m1, m2, m3 = [
        jnp.sum(jnp.where(lane == k, line, 0.0), axis=1, keepdims=True) for k in range(4)
    ]
    a1 = m0 / m1
    left = a1 * a1 * m2 - m0
    grow = 1.0 + left / m0
    a2 = left / (grow * grow * m1 - 2.0 * grow * a1 * m2 + a1 * a1 * m3)
    c0 = jnp.broadcast_to(a1 + a2 * grow, (sub, LANES))
    c1 = jnp.broadcast_to(a1 * a2, (sub, LANES))
    for i in range(3):
        for t in range(layers):
            for w in range(columns):
                out[i, t, pl.ds(w, sub, stride=columns), :] = (
                    c0 * force[i, t, w] - c1 * image[i, t, w]
                )


def call(
    kernel, shapes, scratch=(), hbm=(), count=0, copies=0, aliases=None, cost=None, work=0, limit=VMEM_LIMIT
):
    anywhere, local = pl.BlockSpec(memory_space=pl.ANY), pl.BlockSpec(memory_space=pltpu.VMEM)
    extra = [pltpu.SemaphoreType.DMA((copies,))] if copies else []
    more = {}
    if cost is not None:
        more["cost_estimate"] = pl.CostEstimate(flops=work, transcendentals=0, bytes_accessed=cost)
    return pl.pallas_call(
        kernel,
        out_shape=[jax.ShapeDtypeStruct(s, jnp.float32) for s in shapes],
        in_specs=[anywhere if k in hbm else local for k in range(count)],
        scratch_shapes=[pltpu.VMEM(s, jnp.float32) for s in scratch] + extra,
        input_output_aliases=aliases or {},
        compiler_params=pltpu.CompilerParams(vmem_limit_bytes=limit),
        **more,
    )


def on_device(ends, deviation, velocity, stiffness):
    _, layers, columns, length = deviation.shape
    sub = length // LANES
    dims = (layers, columns, sub)
    rows = columns * sub
    tile = (sub, LANES)
    w_first, w_second, t_first, t_second = swap_pairs(*ends)
    dev, vel, stiff = as_tiles(deviation), as_tiles(velocity), as_tiles(stiffness)

    wa, wb, ta, tb = call(
        functools.partial(pack_kernel, dims, ends),
        [(9, layers, *tile)] * 2 + [(9, rows, LANES)] * 2,
        [(6, layers, rows, LANES), (3, layers, rows, LANES)],
        hbm=(0, 1), count=2, copies=9, limit=PACK_LIMIT,
    )(dev, vel)
    packed = wa
    tb = swap(tb, t_second)
    wb = swap(wb, w_second)
    wa = swap(wa, w_first)
    ta = swap(ta, t_first)

    ext, tau = call(
        functools.partial(inner_kernel, dims),
        [(9, layers + 2, columns + 2, *tile), (6, layers, columns, *tile)],
        hbm=(2,), count=4, cost=12 * 1024 * 1024,
    )(dev, vel, packed, stiff)

    (tau,) = call(
        functools.partial(side_kernel, dims, ends),
        [(6, layers, columns, *tile)],
        count=4, aliases={0: 0}, cost=1024 * 1024, work=10**10,
    )(tau, ext, wa, wb)

    face = 6 * (layers + 1) + layers
    tau, part, sa, sb = call(
        functools.partial(outer_kernel, dims, ends),
        [(6, layers, columns, *tile), (3, layers + 1, 4, *tile)] + [(face, *tile)] * 2,
        count=5, aliases={0: 0},
    )(tau, ext, ta, tb, stiff)
    wb = swap(sb, w_second)
    wa = swap(sa, w_first)

    broad = 6 * (columns - 1) + columns
    mid, sa, sb = call(
        functools.partial(middle_kernel, dims, ends),
        [(3, layers + 1, columns - 1, *tile)] + [(broad, *tile)] * 2,
        count=3, cost=2 * 1024 * 1024,
    )(tau, part, stiff)
    mb = swap(sb, t_second)
    ma = swap(sa, t_first)

    side, sa, sb = call(
        functools.partial(join_kernel, dims, ends),
        [(3, layers + 1, 4, *tile)] + [(24, *tile)] * 2,
        count=3,
    )(part, wb, wa)
    jb = swap(sb, t_second)
    ja = swap(sa, t_first)

    new, done = call(
        functools.partial(emit_kernel, dims), [(6, layers, rows, LANES), tile],
        hbm=(1,), count=2, cost=6 * 1024 * 1024,
    )(tau, side)

    force, image, sums = call(
        functools.partial(krylov_kernel, dims, ends),
        [(3, layers, columns, *tile)] * 2 + [(ends[0] * ends[1], 1, LANES)],
        [(3, layers + 3, columns + 3, *tile), (3, layers + 1, columns + 1, *tile)],
        count=10,
    )(mid, side, mb, ma, jb, ja, wa, wb, stiff, done)
    sums = lax.all_to_all(sums, AXES, 0, 0, tiled=True)

    (out,) = call(
        functools.partial(finish_kernel, dims), [(3, layers, rows, LANES)], count=3
    )(sums, force, image)
    return from_tiles(new, columns), from_tiles(out, columns)


def solution(mesh):
    placed = (
        P(None, "thick", "width", None),
        P(None, "thick", "width", None),
        P("thick", "width", None),
    )
    ends = (mesh.shape["width"], mesh.shape["thick"])
    return jax.shard_map(
        functools.partial(on_device, ends),
        mesh=mesh,
        in_specs=placed,
        out_specs=(P(None, "thick", "width", None), P(None, "thick", "width", None)),
        check_vma=False,
    )
```

```python
import functools

import jax
import jax.numpy as jnp
from jax import lax
from jax.experimental import pallas as pl
from jax.experimental.pallas import tpu as pltpu
from jax.sharding import PartitionSpec as P

TIME_STEP = 0.1
RELAX_TIME = 1.0
MOBILITY = 0.3
MODULUS = 10.0
LANES = 128
AXES = ("width", "thick")
PAIRS = ((0, 0), (1, 1), (2, 2), (0, 1), (0, 2), (1, 2))
SLOT = ((0, 3, 4), (3, 1, 5), (4, 5, 2))
VMEM_LIMIT = 40 * 1024 * 1024
PACK_LIMIT = 53 * 1024 * 1024


def swap_pairs(wide, thick):
    def flat(fn):
        return [
            (w * thick + t, fn(w, t)[0] * thick + fn(w, t)[1])
            for w in range(wide)
            for t in range(thick)
        ]

    def width_second(w, t):
        return (w, t ^ 1) if w in (0, wide - 1) else (((w - 1) ^ 1) + 1, t)

    def thick_second(w, t):
        return (w ^ 2, t) if t in (0, thick - 1) else (w, ((t - 1) ^ 1) + 1)

    def thick_across(w, t):
        return (w, thick - 1 - t) if t in (0, thick - 1) else (w, ((t - 1) ^ 1) + 1)

    return (
        flat(lambda w, t: (w ^ 1, t)),
        flat(width_second),
        flat(lambda w, t: (w, t ^ 1)),
        flat(thick_second),
        flat(thick_across),
    )


def swap(value, pairs):
    return lax.ppermute(value, AXES, pairs)


def as_tiles(x):
    *lead, w, length = x.shape
    x = x.reshape(*lead, w, length // LANES, LANES)
    return jnp.swapaxes(x, -3, -2).reshape(*lead, length // LANES * w, LANES)


def from_tiles(x, w):
    *lead, rows, lanes = x.shape
    x = x.reshape(*lead, rows // w, w, lanes)
    return jnp.swapaxes(x, -3, -2).reshape(*lead, w, rows // w * lanes)


def row_of(ref, lead, w, columns, sub):
    return ref[(*lead, pl.ds(w, sub, stride=columns), slice(None))]


def edge_masks(sub):
    lane = lax.broadcasted_iota(jnp.int32, (sub, LANES), 1)
    row = lax.broadcasted_iota(jnp.int32, (sub, LANES), 0)
    first, last = lane == 0, lane == LANES - 1
    return first, first & (row == 0), last, last & (row == sub - 1)


def before(x, masks):
    first, corner = masks[0], masks[1]
    near = pltpu.roll(x, 1, axis=1)
    far = pltpu.roll(near, 1, axis=0)
    return jnp.where(corner, 0.0, jnp.where(first, far, near))


def after(x, masks):
    last, corner = masks[2], masks[3]
    sub = x.shape[0]
    near = pltpu.roll(x, LANES - 1, axis=1)
    far = pltpu.roll(near, sub - 1, axis=0)
    return jnp.where(corner, 0.0, jnp.where(last, far, near))


def halves(axis, end):
    at = lax.axis_index(axis)
    even = at % 2 == 0
    has_low, has_high = at > 0, at < end - 1

    def low(first, second):
        return jnp.where(has_low, jnp.where(even, second, first), 0.0)

    def high(first, second):
        return jnp.where(has_high, jnp.where(even, first, second), 0.0)

    def send(low_face, high_face):
        return jnp.where(even, high_face, low_face), jnp.where(even, low_face, high_face)

    return low, high, send, has_high


def fetch(sources, targets, sems):
    copies = []
    for source, target in zip(sources, targets):
        for c in range(source.shape[0]):
            copies.append(pltpu.make_async_copy(source.at[c], target.at[c], sems.at[len(copies)]))
    for copy in copies:
        copy.start()
    for copy in copies:
        copy.wait()


def pack_kernel(dims, ends, dev_hbm, vel_hbm, wa, wb, ta, tb, dev, vel, sems):
    layers, columns, sub = dims
    send_w = halves("width", ends[0])[2]
    send_t = halves("thick", ends[1])[2]
    fetch((dev_hbm, vel_hbm), (dev, vel), sems)
    for c in range(9):
        ref, lead = (dev, (c,)) if c < 6 else (vel, (c - 6,))
        for t in range(layers):
            low = row_of(ref, (*lead, t), 0, columns, sub)
            high = row_of(ref, (*lead, t), columns - 1, columns, sub)
            wa[c, t], wb[c, t] = send_w(low, high)
        ta[c], tb[c] = send_t(ref[(*lead, 0)], ref[(*lead, layers - 1)])


HALF = 0.5 * TIME_STEP


def inner_kernel(dims, dev, vel, after_pack, stiff, ext, tau):
    layers, columns, sub = dims
    masks = edge_masks(sub)
    zero = jnp.zeros((sub, LANES), jnp.float32)
    for c in range(9):
        ref, lead = (dev, (c,)) if c < 6 else (vel, (c - 6,))
        for t in range(layers):
            for w in range(columns):
                ext[c, t + 1, w + 1] = row_of(ref, (*lead, t), w, columns, sub)
            ext[c, t + 1, 0] = zero
            ext[c, t + 1, columns + 1] = zero
        for w in range(columns):
            ext[c, 0, w + 1] = zero
            ext[c, layers + 1, w + 1] = zero

    def cell(t, w):
        def at(c, d, off):
            where = [t + 1, w + 1]
            where[d] = where[d] + off
            return ext[c, where[0], where[1]]

        s = [ext[c, t + 1, w + 1] for c in range(6)]
        u = [ext[6 + c, t + 1, w + 1] for c in range(3)]
        grad = [
            [HALF * (at(6 + i, j, 1) - at(6 + i, j, -1)) for j in range(2)]
            + [HALF * (after(u[i], masks) - before(u[i], masks))]
            for i in range(3)
        ]
        pos = [TIME_STEP * jnp.maximum(u[d], 0.0) for d in range(3)]
        neg = [TIME_STEP * jnp.minimum(u[d], 0.0) for d in range(3)]
        keep = (1.0 - TIME_STEP / RELAX_TIME) - (
            (pos[0] - neg[0]) + (pos[1] - neg[1]) + (pos[2] - neg[2])
        )
        bend = HALF * MOBILITY / RELAX_TIME
        scaled = [bend * s[c] for c in range(6)]
        turn = [[grad[i][k] - scaled[SLOT[i][k]] for k in range(3)] for i in range(3)]
        for p, (i, j) in enumerate(PAIRS):
            out = keep * s[p]
            for d in range(2):
                out = out + pos[d] * at(p, d, -1) - neg[d] * at(p, d, 1)
            out = out + pos[2] * before(s[p], masks) - neg[2] * after(s[p], masks)
            if i == j:
                more = grad[i][i]
                for k in range(3):
                    more = more + turn[i][k] * s[SLOT[k][i]]
                out = out + 2.0 * more
            else:
                out = out + (grad[i][j] + grad[j][i])
                for k in range(3):
                    out = out + turn[i][k] * s[SLOT[k][j]] + turn[j][k] * s[SLOT[k][i]]
            tau[p, t, w] = out

    def cells(step, carry):
        t, w = step // (columns // 2), step % (columns // 2)
        cell(t, 2 * w)
        cell(t, 2 * w + 1)
        return carry

    lax.fori_loop(0, layers * columns // 2, cells, 0)


def nodes(dims, tau, columns_of_nodes, put):
    layers, columns, sub = dims
    masks = edge_masks(sub)
    scale = 0.25 * MODULUS
    for w in columns_of_nodes:
        lower = None
        for t in range(layers + 1):
            level = []
            if t < layers:
                here = [tau[c, t, w] for c in range(6)] if w < columns else None
                back = [tau[c, t, w - 1] for c in range(6)] if w > 0 else None
                if here is None:
                    total, delta = back, [-x for x in back]
                elif back is None:
                    total = delta = here
                else:
                    total = [a + b for a, b in zip(here, back)]
                    delta = [a - b for a, b in zip(here, back)]
                for i in range(3):
                    m, q = delta[SLOT[i][1]], total[SLOT[i][2]]
                    level.append((total[SLOT[i][0]], m + q, m - q))
            for i in range(3):
                if t < layers:
                    x, y, z = level[i]
                    plus, minus = x + y, x + z
                    if t > 0:
                        plus, minus = plus + lower[i][0], minus + lower[i][1]
                else:
                    plus, minus = lower[i]
                put(i, t, w, scale * (plus + before(minus, masks)))
            lower = [(y - x, z - x) for x, y, z in level]


def correct(tau, ext, t, w, d, sign, halo):
    s = [ext[c, t + 1, w + 1] for c in range(6)]
    u = ext[6 + d, t + 1, w + 1]
    speed = TIME_STEP * (jnp.maximum(u, 0.0) if sign < 0 else -jnp.minimum(u, 0.0))
    h = [(sign * HALF) * halo[6 + i] for i in range(3)]
    q = [s[SLOT[d][j]] for j in range(3)]
    q[d] = q[d] + 1.0
    for p, (i, j) in enumerate(PAIRS):
        bent = 2.0 * (h[i] * q[i]) if i == j else h[i] * q[j] + h[j] * q[i]
        tau[p, t, w] = tau[p, t, w] + (speed * halo[p] + bent)


def side_kernel(dims, ends, tau_in, ext, wa, wb, tau):
    layers, columns, sub = dims
    w_low, w_high, _, _ = halves("width", ends[0])

    def side(t, carry):
        a, b = [wa[c, t] for c in range(9)], [wb[c, t] for c in range(9)]
        correct(tau, ext, t, 0, 1, -1.0, [w_low(x, y) for x, y in zip(a, b)])
        correct(tau, ext, t, columns - 1, 1, 1.0, [w_high(x, y) for x, y in zip(a, b)])
        return carry

    lax.fori_loop(0, layers, side, 0)


def outer_kernel(dims, ends, tau_in, ext, ta, tb, stiff, tau, part, sa, sb):
    layers, columns, sub = dims
    send_w = halves("width", ends[0])[2]
    t_low, t_high, _, _ = halves("thick", ends[1])
    for w in range(columns):
        a = [row_of(ta, (c,), w, columns, sub) for c in range(9)]
        b = [row_of(tb, (c,), w, columns, sub) for c in range(9)]
        correct(tau, ext, 0, w, 0, -1.0, [t_low(x, y) for x, y in zip(a, b)])
        correct(tau, ext, layers - 1, w, 0, 1.0, [t_high(x, y) for x, y in zip(a, b)])

    slot = {0: 0, 1: 1, columns - 1: 2, columns: 3}

    def put(i, t, w, value):
        part[i, t, slot[w]] = value

    nodes(dims, tau, slot, put)
    count = 2 * (layers + 1)
    for i in range(3):
        for t in range(layers + 1):
            for k in range(2):
                at = i * count + t * 2 + k
                sa[at], sb[at] = send_w(part[i, t, k], part[i, t, 2 + k])
    for t in range(layers):
        row = row_of(stiff, (t,), 0, columns, sub)
        sa[3 * count + t] = row
        sb[3 * count + t] = row


def middle_kernel(dims, ends, tau, part, stiff, mid, sa, sb):
    layers, columns, sub = dims
    send_t = halves("thick", ends[1])[2]

    def put(i, t, w, value):
        mid[i, t, w - 1] = value

    nodes(dims, tau, range(2, columns - 1), put)
    for i in range(3):
        for t in range(layers + 1):
            mid[i, t, 0] = part[i, t, 1]
            mid[i, t, columns - 2] = part[i, t, 2]
    inner = columns - 1
    for i in range(3):
        for k in range(2):
            for w in range(inner):
                at = (i * 2 + k) * inner + w
                sa[at], sb[at] = send_t(mid[i, k, w], mid[i, layers - 1 + k, w])
    for w in range(columns):
        row = row_of(stiff, (0,), w, columns, sub)
        sa[6 * inner + w] = row
        sb[6 * inner + w] = row


def emit_kernel(dims, tau, after_join, new, done):
    layers, columns, sub = dims
    done[...] = jnp.zeros_like(done)
    for c in range(6):
        for t in range(layers):
            for w in range(columns):
                new[c, t, pl.ds(w, sub, stride=columns), :] = tau[c, t, w]


def join_kernel(dims, ends, part, wa, wb, side, sa, sb):
    layers, columns, sub = dims
    w_low, w_high, _, has_high = halves("width", ends[0])
    send_t = halves("thick", ends[1])[2]
    count = 2 * (layers + 1)
    for i in range(3):
        for t in range(layers + 1):
            at = i * count + t * 2
            below = [w_low(wa[at + k], wb[at + k]) for k in range(2)]
            above = [w_high(wa[at + k], wb[at + k]) for k in range(2)]
            side[i, t, 0] = below[0]
            side[i, t, 1] = part[i, t, 0] + below[1]
            side[i, t, 2] = jnp.where(has_high, part[i, t, 3] + above[0], 0.0)
            side[i, t, 3] = above[1]
    for i in range(3):
        for k in range(2):
            for w in range(4):
                at = (i * 2 + k) * 4 + w
                sa[at], sb[at] = send_t(side[i, k, w], side[i, layers - 1 + k, w])


def krylov_kernel(
    dims, ends, mid, side, mb, ma, jb, ja, wa, wb, stiff, after_emit, force, image, sums, ext, img
):
    layers, columns, sub = dims
    w_high = halves("width", ends[0])[1]
    has_right = halves("width", ends[0])[3]
    t_low, t_high, _, has_top = halves("thick", ends[1])
    masks = edge_masks(sub)
    zero = jnp.zeros((sub, LANES), jnp.float32)
    inner = columns - 1
    edge = {0: 0, 1: 1, columns + 1: 2, columns + 2: 3}
    for i in range(3):
        for w in range(columns + 3):
            if w in edge:
                own, a, b, at, step = side, ja, jb, edge[w], 4
            else:
                own, a, b, at, step = mid, ma, mb, w - 2, inner
            a = [a[(i * 2 + k) * step + at] for k in range(2)]
            b = [b[(i * 2 + k) * step + at] for k in range(2)]
            below = [t_low(x, y) for x, y in zip(a, b)]
            above = [t_high(x, y) for x, y in zip(a, b)]
            ext[i, 0, w] = below[0]
            ext[i, 1, w] = own[i, 0, at] + below[1]
            for t in range(1, layers):
                ext[i, t + 1, w] = own[i, t, at]
            ext[i, layers + 1, w] = jnp.where(has_top, own[i, layers, at] + above[0], 0.0)
            ext[i, layers + 2, w] = above[1]

    def apply(i, t, w, diagonal):
        here = ext[i, t + 1, w + 1]
        beside = ext[i, t, w + 1] + ext[i, t + 2, w + 1]
        beside = beside + (ext[i, t + 1, w] + ext[i, t + 1, w + 2])
        beside = beside + (before(here, masks) + after(here, masks))
        return here, diagonal * here - beside

    count = 2 * (layers + 1)
    for t in range(layers):
        d = 6.0 + w_high(wa[3 * count + t], wb[3 * count + t])
        for i in range(3):
            _, g = apply(i, t, columns, d)
            img[i, t, columns] = jnp.where(has_right, g, 0.0)
    for w in range(columns):
        d = 6.0 + t_high(ma[6 * inner + w], mb[6 * inner + w])
        for i in range(3):
            _, g = apply(i, layers, w, d)
            img[i, layers, w] = jnp.where(has_top, g, 0.0)
    for t in range(layers):
        for w in range(columns):
            d = 6.0 + row_of(stiff, (t,), w, columns, sub)
            for i in range(3):
                f, g = apply(i, t, w, d)
                img[i, t, w] = g
                image[i, t, w] = g
                force[i, t, w] = f
    m0 = m1 = m2 = m3 = me = zero
    for t in range(layers):
        for w in range(columns):
            d = 6.0 + row_of(stiff, (t,), w, columns, sub)
            square = zero
            for i in range(3):
                f, g = ext[i, t + 1, w + 1], img[i, t, w]
                m0, m1 = m0 + f * f, m1 + f * g
                square = square + g * g
                me = me + g * (img[i, t + 1, w] + img[i, t, w + 1] + after(g, masks))
            m2, m3 = m2 + square, m3 + d * square
    m3 = m3 - 2.0 * me
    lane = lax.broadcasted_iota(jnp.int32, (1, LANES), 1)
    line = jnp.zeros((1, LANES), jnp.float32)
    for k, m in enumerate((m0, m1, m2, m3)):
        line = jnp.where(lane == k, jnp.sum(m, keepdims=True), line)
    sums[...] = jnp.broadcast_to(line[None], sums.shape)


def finish_kernel(dims, sums, force, image, out):
    layers, columns, sub = dims
    line = jnp.sum(sums[...], axis=0)
    lane = lax.broadcasted_iota(jnp.int32, (1, LANES), 1)
    m0, m1, m2, m3 = [
        jnp.sum(jnp.where(lane == k, line, 0.0), axis=1, keepdims=True) for k in range(4)
    ]
    a1 = m0 / m1
    left = a1 * a1 * m2 - m0
    grow = 1.0 + left / m0
    a2 = left / (grow * grow * m1 - 2.0 * grow * a1 * m2 + a1 * a1 * m3)
    c0 = jnp.broadcast_to(a1 + a2 * grow, (sub, LANES))
    c1 = jnp.broadcast_to(a1 * a2, (sub, LANES))
    for i in range(3):
        for t in range(layers):
            for w in range(columns):
                out[i, t, pl.ds(w, sub, stride=columns), :] = (
                    c0 * force[i, t, w] - c1 * image[i, t, w]
                )


def call(
    kernel, shapes, scratch=(), hbm=(), count=0, copies=0, aliases=None, cost=None, work=0, limit=VMEM_LIMIT
):
    anywhere, local = pl.BlockSpec(memory_space=pl.ANY), pl.BlockSpec(memory_space=pltpu.VMEM)
    extra = [pltpu.SemaphoreType.DMA((copies,))] if copies else []
    more = {}
    if cost is not None:
        more["cost_estimate"] = pl.CostEstimate(flops=work, transcendentals=0, bytes_accessed=cost)
    return pl.pallas_call(
        kernel,
        out_shape=[jax.ShapeDtypeStruct(s, jnp.float32) for s in shapes],
        in_specs=[anywhere if k in hbm else local for k in range(count)],
        scratch_shapes=[pltpu.VMEM(s, jnp.float32) for s in scratch] + extra,
        input_output_aliases=aliases or {},
        compiler_params=pltpu.CompilerParams(vmem_limit_bytes=limit),
        **more,
    )


def on_device(ends, deviation, velocity, stiffness):
    _, layers, columns, length = deviation.shape
    sub = length // LANES
    dims = (layers, columns, sub)
    rows = columns * sub
    tile = (sub, LANES)
    w_first, w_second, t_first, t_second, t_across = swap_pairs(*ends)
    dev, vel, stiff = as_tiles(deviation), as_tiles(velocity), as_tiles(stiffness)

    wa, wb, ta, tb = call(
        functools.partial(pack_kernel, dims, ends),
        [(9, layers, *tile)] * 2 + [(9, rows, LANES)] * 2,
        [(6, layers, rows, LANES), (3, layers, rows, LANES)],
        hbm=(0, 1), count=2, copies=9, limit=PACK_LIMIT,
    )(dev, vel)
    packed = wa
    tb = swap(tb, t_second)
    wb = swap(wb, w_second)
    wa = swap(wa, w_first)
    ta = swap(ta, t_first)

    ext, tau = call(
        functools.partial(inner_kernel, dims),
        [(9, layers + 2, columns + 2, *tile), (6, layers, columns, *tile)],
        hbm=(2,), count=4, cost=12 * 1024 * 1024,
    )(dev, vel, packed, stiff)

    (tau,) = call(
        functools.partial(side_kernel, dims, ends),
        [(6, layers, columns, *tile)],
        count=4, aliases={0: 0}, cost=1024 * 1024, work=10**10,
    )(tau, ext, wa, wb)

    face = 6 * (layers + 1) + layers
    tau, part, sa, sb = call(
        functools.partial(outer_kernel, dims, ends),
        [(6, layers, columns, *tile), (3, layers + 1, 4, *tile)] + [(face, *tile)] * 2,
        count=5, aliases={0: 0},
    )(tau, ext, ta, tb, stiff)
    wb = swap(sb, w_second)
    wa = swap(sa, w_first)

    broad = 6 * (columns - 1) + columns
    mid, sa, sb = call(
        functools.partial(middle_kernel, dims, ends),
        [(3, layers + 1, columns - 1, *tile)] + [(broad, *tile)] * 2,
        count=3, cost=2 * 1024 * 1024,
    )(tau, part, stiff)
    mb = swap(sb, t_across)
    ma = swap(sa, t_first)

    side, sa, sb = call(
        functools.partial(join_kernel, dims, ends),
        [(3, layers + 1, 4, *tile)] + [(24, *tile)] * 2,
        count=3,
    )(part, wa, wb)
    jb = swap(sb, t_second)
    ja = swap(sa, t_first)

    new, done = call(
        functools.partial(emit_kernel, dims), [(6, layers, rows, LANES), tile],
        hbm=(1,), count=2, cost=6 * 1024 * 1024,
    )(tau, side)

    force, image, sums = call(
        functools.partial(krylov_kernel, dims, ends),
        [(3, layers, columns, *tile)] * 2 + [(ends[0] * ends[1], 1, LANES)],
        [(3, layers + 3, columns + 3, *tile), (3, layers + 1, columns + 1, *tile)],
        count=10,
    )(mid, side, mb, ma, jb, ja, wa, wb, stiff, done)
    sums = lax.all_to_all(sums, AXES, 0, 0, tiled=True)

    (out,) = call(
        functools.partial(finish_kernel, dims), [(3, layers, rows, LANES)], count=3
    )(sums, force, image)
    return from_tiles(new, columns), from_tiles(out, columns)


def solution(mesh):
    placed = (
        P(None, "thick", "width", None),
        P(None, "thick", "width", None),
        P("thick", "width", None),
    )
    ends = (mesh.shape["width"], mesh.shape["thick"])
    return jax.shard_map(
        functools.partial(on_device, ends),
        mesh=mesh,
        in_specs=placed,
        out_specs=(P(None, "thick", "width", None), P(None, "thick", "width", None)),
        check_vma=False,
    )
```

```python
import functools

import jax
import jax.numpy as jnp
from jax import lax
from jax.experimental import pallas as pl
from jax.experimental.pallas import tpu as pltpu
from jax.sharding import PartitionSpec as P

TIME_STEP = 0.1
RELAX_TIME = 1.0
MOBILITY = 0.3
MODULUS = 10.0
LANES = 128
AXES = ("width", "thick")
PAIRS = ((0, 0), (1, 1), (2, 2), (0, 1), (0, 2), (1, 2))
SLOT = ((0, 3, 4), (3, 1, 5), (4, 5, 2))
VMEM_LIMIT = 40 * 1024 * 1024


def swap_pairs(wide, thick):
    def flat(fn):
        return [
            (w * thick + t, fn(w, t)[0] * thick + fn(w, t)[1])
            for w in range(wide)
            for t in range(thick)
        ]

    def width_second(w, t):
        return (w, t ^ 1) if w in (0, wide - 1) else (((w - 1) ^ 1) + 1, t)

    def thick_second(w, t):
        return (w ^ 2, t) if t in (0, thick - 1) else (w, ((t - 1) ^ 1) + 1)

    def thick_across(w, t):
        return (w, thick - 1 - t) if t in (0, thick - 1) else (w, ((t - 1) ^ 1) + 1)

    return (
        flat(lambda w, t: (w ^ 1, t)),
        flat(width_second),
        flat(lambda w, t: (w, t ^ 1)),
        flat(thick_second),
        flat(thick_across),
        [p for p in flat(thick_across) if p[0] % thick not in (0, thick - 1)],
    )


def swap(value, pairs):
    return lax.ppermute(value, AXES, pairs)


def as_tiles(x):
    *lead, w, length = x.shape
    x = x.reshape(*lead, w, length // LANES, LANES)
    return jnp.swapaxes(x, -3, -2).reshape(*lead, length // LANES * w, LANES)


def from_tiles(x, w):
    *lead, rows, lanes = x.shape
    x = x.reshape(*lead, rows // w, w, lanes)
    return jnp.swapaxes(x, -3, -2).reshape(*lead, w, rows // w * lanes)


def row_of(ref, lead, w, columns, sub):
    return ref[(*lead, pl.ds(w, sub, stride=columns), slice(None))]


def edge_masks(sub):
    lane = lax.broadcasted_iota(jnp.int32, (sub, LANES), 1)
    row = lax.broadcasted_iota(jnp.int32, (sub, LANES), 0)
    first, last = lane == 0, lane == LANES - 1
    return first, first & (row == 0), last, last & (row == sub - 1)


def before(x, masks):
    first, corner = masks[0], masks[1]
    near = pltpu.roll(x, 1, axis=1)
    far = pltpu.roll(near, 1, axis=0)
    return jnp.where(corner, 0.0, jnp.where(first, far, near))


def after(x, masks):
    last, corner = masks[2], masks[3]
    sub = x.shape[0]
    near = pltpu.roll(x, LANES - 1, axis=1)
    far = pltpu.roll(near, sub - 1, axis=0)
    return jnp.where(corner, 0.0, jnp.where(last, far, near))


def halves(axis, end):
    at = lax.axis_index(axis)
    even = at % 2 == 0
    has_low, has_high = at > 0, at < end - 1

    def low(first, second):
        return jnp.where(has_low, jnp.where(even, second, first), 0.0)

    def high(first, second):
        return jnp.where(has_high, jnp.where(even, first, second), 0.0)

    def send(low_face, high_face):
        return jnp.where(even, high_face, low_face), jnp.where(even, low_face, high_face)

    return low, high, send, has_high


def fetch(sources, targets, sems):
    copies = []
    for source, target in zip(sources, targets):
        for c in range(source.shape[0]):
            copies.append(pltpu.make_async_copy(source.at[c], target.at[c], sems.at[len(copies)]))
    for copy in copies:
        copy.start()
    return copies


def pack_kernel(
    dims, ends, dev_hbm, vel_hbm, stiff_hbm, wa, wb, ta, tb, stiff, dev, vel, sems
):
    layers, columns, sub = dims
    send_w = halves("width", ends[0])[2]
    send_t = halves("thick", ends[1])[2]
    copies = fetch((dev_hbm, vel_hbm, stiff_hbm), (dev, vel, stiff), sems)
    for c in range(9):
        ref, lead = (dev, (c,)) if c < 6 else (vel, (c - 6,))
        copies[c].wait()
        for t in range(layers):
            low = row_of(ref, (*lead, t), 0, columns, sub)
            high = row_of(ref, (*lead, t), columns - 1, columns, sub)
            wa[c, t], wb[c, t] = send_w(low, high)
        ta[c], tb[c] = send_t(ref[(*lead, 0)], ref[(*lead, layers - 1)])
    for copy in copies[9:]:
        copy.wait()


HALF = 0.5 * TIME_STEP


def inner_kernel(dims, dev, vel, ext, tau):
    layers, columns, sub = dims
    masks = edge_masks(sub)
    zero = jnp.zeros((sub, LANES), jnp.float32)
    for c in range(9):
        ref, lead = (dev, (c,)) if c < 6 else (vel, (c - 6,))
        for t in range(layers):
            for w in range(columns):
                ext[c, t + 1, w + 1] = row_of(ref, (*lead, t), w, columns, sub)
            ext[c, t + 1, 0] = zero
            ext[c, t + 1, columns + 1] = zero
        for w in range(columns):
            ext[c, 0, w + 1] = zero
            ext[c, layers + 1, w + 1] = zero

    def cell(t, w):
        def at(c, d, off):
            where = [t + 1, w + 1]
            where[d] = where[d] + off
            return ext[c, where[0], where[1]]

        s = [ext[c, t + 1, w + 1] for c in range(6)]
        u = [ext[6 + c, t + 1, w + 1] for c in range(3)]
        grad = [
            [HALF * (at(6 + i, j, 1) - at(6 + i, j, -1)) for j in range(2)]
            + [HALF * (after(u[i], masks) - before(u[i], masks))]
            for i in range(3)
        ]
        pos = [TIME_STEP * jnp.maximum(u[d], 0.0) for d in range(3)]
        neg = [TIME_STEP * jnp.minimum(u[d], 0.0) for d in range(3)]
        keep = (1.0 - TIME_STEP / RELAX_TIME) - (
            (pos[0] - neg[0]) + (pos[1] - neg[1]) + (pos[2] - neg[2])
        )
        bend = HALF * MOBILITY / RELAX_TIME
        scaled = [bend * s[c] for c in range(6)]
        turn = [[grad[i][k] - scaled[SLOT[i][k]] for k in range(3)] for i in range(3)]
        for p, (i, j) in enumerate(PAIRS):
            out = keep * s[p]
            for d in range(2):
                out = out + pos[d] * at(p, d, -1) - neg[d] * at(p, d, 1)
            out = out + pos[2] * before(s[p], masks) - neg[2] * after(s[p], masks)
            if i == j:
                more = grad[i][i]
                for k in range(3):
                    more = more + turn[i][k] * s[SLOT[k][i]]
                out = out + 2.0 * more
            else:
                out = out + (grad[i][j] + grad[j][i])
                for k in range(3):
                    out = out + turn[i][k] * s[SLOT[k][j]] + turn[j][k] * s[SLOT[k][i]]
            tau[p, t, w] = out

    def cells(step, carry):
        t, w = step // (columns // 2), step % (columns // 2)
        cell(t, 2 * w)
        cell(t, 2 * w + 1)
        return carry

    lax.fori_loop(0, layers * columns // 2, cells, 0)


def nodes(dims, tau, columns_of_nodes, put):
    layers, columns, sub = dims
    masks = edge_masks(sub)
    scale = 0.25 * MODULUS
    for w in columns_of_nodes:
        lower = None
        for t in range(layers + 1):
            level = []
            if t < layers:
                here = [tau[c, t, w] for c in range(6)] if w < columns else None
                back = [tau[c, t, w - 1] for c in range(6)] if w > 0 else None
                if here is None:
                    total, delta = back, [-x for x in back]
                elif back is None:
                    total = delta = here
                else:
                    total = [a + b for a, b in zip(here, back)]
                    delta = [a - b for a, b in zip(here, back)]
                for i in range(3):
                    m, q = delta[SLOT[i][1]], total[SLOT[i][2]]
                    level.append((total[SLOT[i][0]], m + q, m - q))
            for i in range(3):
                if t < layers:
                    x, y, z = level[i]
                    plus, minus = x + y, x + z
                    if t > 0:
                        plus, minus = plus + lower[i][0], minus + lower[i][1]
                else:
                    plus, minus = lower[i]
                put(i, t, w, scale * (plus + before(minus, masks)))
            lower = [(y - x, z - x) for x, y, z in level]


def correct(tau, ext, t, w, d, sign, halo):
    s = [ext[c, t + 1, w + 1] for c in range(6)]
    u = ext[6 + d, t + 1, w + 1]
    speed = TIME_STEP * (jnp.maximum(u, 0.0) if sign < 0 else -jnp.minimum(u, 0.0))
    h = [(sign * HALF) * halo[6 + i] for i in range(3)]
    q = [s[SLOT[d][j]] for j in range(3)]
    q[d] = q[d] + 1.0
    for p, (i, j) in enumerate(PAIRS):
        bent = 2.0 * (h[i] * q[i]) if i == j else h[i] * q[j] + h[j] * q[i]
        tau[p, t, w] = tau[p, t, w] + (speed * halo[p] + bent)


def side_kernel(dims, ends, tau_in, ext, wa, wb, tau):
    layers, columns, sub = dims
    w_low, w_high, _, _ = halves("width", ends[0])

    def side(t, carry):
        a, b = [wa[c, t] for c in range(9)], [wb[c, t] for c in range(9)]
        correct(tau, ext, t, 0, 1, -1.0, [w_low(x, y) for x, y in zip(a, b)])
        correct(tau, ext, t, columns - 1, 1, 1.0, [w_high(x, y) for x, y in zip(a, b)])
        return carry

    lax.fori_loop(0, layers, side, 0)


def outer_kernel(dims, ends, tau_in, ext, ta, tb, stiff, tau, part, sa, sb):
    layers, columns, sub = dims
    send_w = halves("width", ends[0])[2]
    t_low, t_high, _, _ = halves("thick", ends[1])
    for w in range(columns):
        a = [row_of(ta, (c,), w, columns, sub) for c in range(9)]
        b = [row_of(tb, (c,), w, columns, sub) for c in range(9)]
        correct(tau, ext, 0, w, 0, -1.0, [t_low(x, y) for x, y in zip(a, b)])
        correct(tau, ext, layers - 1, w, 0, 1.0, [t_high(x, y) for x, y in zip(a, b)])

    slot = {0: 0, 1: 1, columns - 1: 2, columns: 3}

    def put(i, t, w, value):
        part[i, t, slot[w]] = value

    nodes(dims, tau, slot, put)
    count = 2 * (layers + 1)
    for i in range(3):
        for t in range(layers + 1):
            for k in range(2):
                at = i * count + t * 2 + k
                sa[at], sb[at] = send_w(part[i, t, k], part[i, t, 2 + k])
    for t in range(layers):
        row = row_of(stiff, (t,), 0, columns, sub)
        sa[3 * count + t] = row
        sb[3 * count + t] = row


def middle_kernel(dims, ends, tau, part, stiff, mid, sa, sb):
    layers, columns, sub = dims
    send_t = halves("thick", ends[1])[2]

    def put(i, t, w, value):
        mid[i, t, w - 1] = value

    nodes(dims, tau, range(2, columns - 1), put)
    for i in range(3):
        for t in range(layers + 1):
            mid[i, t, 0] = part[i, t, 1]
            mid[i, t, columns - 2] = part[i, t, 2]
    inner = columns - 1
    for i in range(3):
        for k in range(2):
            for w in range(inner):
                at = (i * 2 + k) * inner + w
                sa[at], sb[at] = send_t(mid[i, k, w], mid[i, layers - 1 + k, w])
    for w in range(columns):
        row = row_of(stiff, (0,), w, columns, sub)
        sa[6 * inner + w] = row
        sb[6 * inner + w] = row


def emit_kernel(dims, tau, after_join, new, done):
    layers, columns, sub = dims
    done[...] = jnp.zeros_like(done)
    for c in range(6):
        for t in range(layers):
            for w in range(columns):
                new[c, t, pl.ds(w, sub, stride=columns), :] = tau[c, t, w]


def join_kernel(dims, ends, part, wa, wb, side, sa, sb):
    layers, columns, sub = dims
    w_low, w_high, _, has_high = halves("width", ends[0])
    send_t = halves("thick", ends[1])[2]
    count = 2 * (layers + 1)
    for i in range(3):
        for t in range(layers + 1):
            at = i * count + t * 2
            below = [w_low(wa[at + k], wb[at + k]) for k in range(2)]
            above = [w_high(wa[at + k], wb[at + k]) for k in range(2)]
            side[i, t, 0] = below[0]
            side[i, t, 1] = part[i, t, 0] + below[1]
            side[i, t, 2] = jnp.where(has_high, part[i, t, 3] + above[0], 0.0)
            side[i, t, 3] = above[1]
    for i in range(3):
        for k in range(2):
            for w in range(4):
                at = (i * 2 + k) * 4 + w
                sa[at], sb[at] = send_t(side[i, k, w], side[i, layers - 1 + k, w])


def krylov_kernel(
    dims, ends, mid, side, mb, ma, jb, ja, wa, wb, stiff, after_emit, force, image, sums, ext, img
):
    layers, columns, sub = dims
    w_high = halves("width", ends[0])[1]
    has_right = halves("width", ends[0])[3]
    t_low, t_high, _, has_top = halves("thick", ends[1])
    masks = edge_masks(sub)
    zero = jnp.zeros((sub, LANES), jnp.float32)
    inner = columns - 1
    edge = {0: 0, 1: 1, columns + 1: 2, columns + 2: 3}
    for i in range(3):
        for w in range(columns + 3):
            if w in edge:
                own, a, b, at, step = side, ja, jb, edge[w], 4
            else:
                own, a, b, at, step = mid, ma, mb, w - 2, inner
            a = [a[(i * 2 + k) * step + at] for k in range(2)]
            b = [b[(i * 2 + k) * step + at] for k in range(2)]
            below = [t_low(x, y) for x, y in zip(a, b)]
            above = [t_high(x, y) for x, y in zip(a, b)]
            ext[i, 0, w] = below[0]
            ext[i, 1, w] = own[i, 0, at] + below[1]
            for t in range(1, layers):
                ext[i, t + 1, w] = own[i, t, at]
            ext[i, layers + 1, w] = jnp.where(has_top, own[i, layers, at] + above[0], 0.0)
            ext[i, layers + 2, w] = above[1]

    def apply(i, t, w, diagonal):
        here = ext[i, t + 1, w + 1]
        beside = ext[i, t, w + 1] + ext[i, t + 2, w + 1]
        beside = beside + (ext[i, t + 1, w] + ext[i, t + 1, w + 2])
        beside = beside + (before(here, masks) + after(here, masks))
        return here, diagonal * here - beside

    count = 2 * (layers + 1)
    for t in range(layers):
        d = 6.0 + w_high(wa[3 * count + t], wb[3 * count + t])
        for i in range(3):
            _, g = apply(i, t, columns, d)
            img[i, t, columns] = jnp.where(has_right, g, 0.0)
    for w in range(columns):
        d = 6.0 + t_high(ma[6 * inner + w], mb[6 * inner + w])
        for i in range(3):
            _, g = apply(i, layers, w, d)
            img[i, layers, w] = jnp.where(has_top, g, 0.0)
    for t in range(layers):
        for w in range(columns):
            d = 6.0 + row_of(stiff, (t,), w, columns, sub)
            for i in range(3):
                f, g = apply(i, t, w, d)
                img[i, t, w] = g
                image[i, t, w] = g
                force[i, t, w] = f
    m0 = m1 = m2 = m3 = me = zero
    for t in range(layers):
        for w in range(columns):
            d = 6.0 + row_of(stiff, (t,), w, columns, sub)
            square = zero
            for i in range(3):
                f, g = ext[i, t + 1, w + 1], img[i, t, w]
                m0, m1 = m0 + f * f, m1 + f * g
                square = square + g * g
                me = me + g * (img[i, t + 1, w] + img[i, t, w + 1] + after(g, masks))
            m2, m3 = m2 + square, m3 + d * square
    m3 = m3 - 2.0 * me
    lane = lax.broadcasted_iota(jnp.int32, (1, LANES), 1)
    line = jnp.zeros((1, LANES), jnp.float32)
    for k, m in enumerate((m0, m1, m2, m3)):
        line = jnp.where(lane == k, jnp.sum(m, keepdims=True), line)
    sums[...] = jnp.broadcast_to(line[None], sums.shape)


def finish_kernel(dims, sums, force, image, out):
    layers, columns, sub = dims
    line = jnp.sum(sums[...], axis=0)
    lane = lax.broadcasted_iota(jnp.int32, (1, LANES), 1)
    m0, m1, m2, m3 = [
        jnp.sum(jnp.where(lane == k, line, 0.0), axis=1, keepdims=True) for k in range(4)
    ]
    a1 = m0 / m1
    left = a1 * a1 * m2 - m0
    grow = 1.0 + left / m0
    a2 = left / (grow * grow * m1 - 2.0 * grow * a1 * m2 + a1 * a1 * m3)
    c0 = jnp.broadcast_to(a1 + a2 * grow, (sub, LANES))
    c1 = jnp.broadcast_to(a1 * a2, (sub, LANES))
    for i in range(3):
        for t in range(layers):
            for w in range(columns):
                out[i, t, pl.ds(w, sub, stride=columns), :] = (
                    c0 * force[i, t, w] - c1 * image[i, t, w]
                )


def call(
    kernel, shapes, scratch=(), hbm=(), count=0, copies=0, aliases=None, cost=None, work=0
):
    anywhere, local = pl.BlockSpec(memory_space=pl.ANY), pl.BlockSpec(memory_space=pltpu.VMEM)
    extra = [pltpu.SemaphoreType.DMA((copies,))] if copies else []
    more = {}
    if cost is not None:
        more["cost_estimate"] = pl.CostEstimate(flops=work, transcendentals=0, bytes_accessed=cost)
    return pl.pallas_call(
        kernel,
        out_shape=[jax.ShapeDtypeStruct(s, jnp.float32) for s in shapes],
        in_specs=[anywhere if k in hbm else local for k in range(count)],
        scratch_shapes=[pltpu.VMEM(s, jnp.float32) for s in scratch] + extra,
        input_output_aliases=aliases or {},
        compiler_params=pltpu.CompilerParams(vmem_limit_bytes=VMEM_LIMIT),
        **more,
    )


def on_device(ends, deviation, velocity, stiffness):
    _, layers, columns, length = deviation.shape
    sub = length // LANES
    dims = (layers, columns, sub)
    rows = columns * sub
    tile = (sub, LANES)
    w_first, w_second, t_first, t_second, t_across, t_missing = swap_pairs(*ends)
    dev, vel, stiff = as_tiles(deviation), as_tiles(velocity), as_tiles(stiffness)

    wa, wb, ta, tb, stiff, dev, vel = call(
        functools.partial(pack_kernel, dims, ends),
        [(9, layers, *tile)] * 2
        + [(9, rows, LANES)] * 2
        + [(layers, rows, LANES), (6, layers, rows, LANES), (3, layers, rows, LANES)],
        hbm=(0, 1, 2), count=3, copies=9 + layers,
    )(*[pltpu.with_memory_space_constraint(x, pltpu.HBM) for x in (dev, vel, stiff)])
    tb = swap(tb, t_missing)
    wb = swap(wb, w_second)
    wa = swap(wa, w_first)
    ta = swap(ta, t_first)

    ext, tau = call(
        functools.partial(inner_kernel, dims),
        [(9, layers + 2, columns + 2, *tile), (6, layers, columns, *tile)],
        count=2, cost=12 * 1024 * 1024,
    )(dev, vel)

    (tau,) = call(
        functools.partial(side_kernel, dims, ends),
        [(6, layers, columns, *tile)],
        count=4, aliases={0: 0}, cost=1024 * 1024, work=10**10,
    )(tau, ext, wa, wb)

    face = 6 * (layers + 1) + layers
    tau, part, sa, sb = call(
        functools.partial(outer_kernel, dims, ends),
        [(6, layers, columns, *tile), (3, layers + 1, 4, *tile)] + [(face, *tile)] * 2,
        count=5, aliases={0: 0},
    )(tau, ext, ta, tb, stiff)
    wb = swap(sb, w_second)
    wa = swap(sa, w_first)

    broad = 6 * (columns - 1) + columns
    mid, sa, sb = call(
        functools.partial(middle_kernel, dims, ends),
        [(3, layers + 1, columns - 1, *tile)] + [(broad, *tile)] * 2,
        count=3, cost=2 * 1024 * 1024,
    )(tau, part, stiff)
    mb = swap(sb, t_across)
    ma = swap(sa, t_first)

    side, sa, sb = call(
        functools.partial(join_kernel, dims, ends),
        [(3, layers + 1, 4, *tile)] + [(24, *tile)] * 2,
        count=3,
    )(part, wa, wb)
    jb = swap(sb, t_second)
    ja = swap(sa, t_first)

    new, done = call(
        functools.partial(emit_kernel, dims), [(6, layers, rows, LANES), tile],
        hbm=(1,), count=2, cost=6 * 1024 * 1024,
    )(tau, side)

    force, image, sums = call(
        functools.partial(krylov_kernel, dims, ends),
        [(3, layers, columns, *tile)] * 2 + [(ends[0] * ends[1], 1, LANES)],
        [(3, layers + 3, columns + 3, *tile), (3, layers + 1, columns + 1, *tile)],
        count=10,
    )(mid, side, mb, ma, jb, ja, wa, wb, stiff, done)
    sums = lax.all_to_all(sums, AXES, 0, 0, tiled=True)

    (out,) = call(
        functools.partial(finish_kernel, dims), [(3, layers, rows, LANES)], count=3
    )(sums, force, image)
    return from_tiles(new, columns), from_tiles(out, columns)


def solution(mesh):
    placed = (
        P(None, "thick", "width", None),
        P(None, "thick", "width", None),
        P("thick", "width", None),
    )
    ends = (mesh.shape["width"], mesh.shape["thick"])
    return jax.shard_map(
        functools.partial(on_device, ends),
        mesh=mesh,
        in_specs=placed,
        out_specs=(P(None, "thick", "width", None), P(None, "thick", "width", None)),
        check_vma=False,
    )
```

```python
import functools

import jax
import jax.numpy as jnp
from jax import lax
from jax.experimental import pallas as pl
from jax.experimental.pallas import tpu as pltpu
from jax.sharding import PartitionSpec as P

TIME_STEP = 0.1
RELAX_TIME = 1.0
MOBILITY = 0.3
MODULUS = 10.0
LANES = 128
AXES = ("width", "thick")
PAIRS = ((0, 0), (1, 1), (2, 2), (0, 1), (0, 2), (1, 2))
SLOT = ((0, 3, 4), (3, 1, 5), (4, 5, 2))
VMEM_LIMIT = 40 * 1024 * 1024


def swap_pairs(wide, thick):
    def flat(fn):
        return [
            (w * thick + t, fn(w, t)[0] * thick + fn(w, t)[1])
            for w in range(wide)
            for t in range(thick)
        ]

    def width_second(w, t):
        return (w, t ^ 1) if w in (0, wide - 1) else (((w - 1) ^ 1) + 1, t)

    def thick_second(w, t):
        return (w ^ 2, t) if t in (0, thick - 1) else (w, ((t - 1) ^ 1) + 1)

    def thick_across(w, t):
        return (w, thick - 1 - t) if t in (0, thick - 1) else (w, ((t - 1) ^ 1) + 1)

    return (
        flat(lambda w, t: (w ^ 1, t)),
        flat(width_second),
        flat(lambda w, t: (w, t ^ 1)),
        flat(thick_second),
        flat(thick_across),
        [p for p in flat(thick_across) if p[0] % thick not in (0, thick - 1)],
    )


def swap(value, pairs):
    return lax.ppermute(value, AXES, pairs)


def as_tiles(x):
    *lead, w, length = x.shape
    x = x.reshape(*lead, w, length // LANES, LANES)
    return jnp.swapaxes(x, -3, -2).reshape(*lead, length // LANES * w, LANES)


def from_tiles(x, w):
    *lead, rows, lanes = x.shape
    x = x.reshape(*lead, rows // w, w, lanes)
    return jnp.swapaxes(x, -3, -2).reshape(*lead, w, rows // w * lanes)


def row_of(ref, lead, w, columns, sub):
    return ref[(*lead, pl.ds(w, sub, stride=columns), slice(None))]


def edge_masks(sub):
    lane = lax.broadcasted_iota(jnp.int32, (sub, LANES), 1)
    row = lax.broadcasted_iota(jnp.int32, (sub, LANES), 0)
    first, last = lane == 0, lane == LANES - 1
    return first, first & (row == 0), last, last & (row == sub - 1)


def before(x, masks):
    first, corner = masks[0], masks[1]
    near = pltpu.roll(x, 1, axis=1)
    far = pltpu.roll(near, 1, axis=0)
    return jnp.where(corner, 0.0, jnp.where(first, far, near))


def after(x, masks):
    last, corner = masks[2], masks[3]
    sub = x.shape[0]
    near = pltpu.roll(x, LANES - 1, axis=1)
    far = pltpu.roll(near, sub - 1, axis=0)
    return jnp.where(corner, 0.0, jnp.where(last, far, near))


def halves(axis, end):
    at = lax.axis_index(axis)
    even = at % 2 == 0
    has_low, has_high = at > 0, at < end - 1

    def low(first, second):
        return jnp.where(has_low, jnp.where(even, second, first), 0.0)

    def high(first, second):
        return jnp.where(has_high, jnp.where(even, first, second), 0.0)

    def send(low_face, high_face):
        return jnp.where(even, high_face, low_face), jnp.where(even, low_face, high_face)

    return low, high, send, has_high


def fetch(sources, targets, sems):
    copies = []
    for source, target in zip(sources, targets):
        copies.append(pltpu.make_async_copy(source, target, sems.at[len(copies)]))
    for copy in copies:
        copy.start()
    return copies


def pack_kernel(
    dims, ends, dev_hbm, vel_hbm, stiff_hbm, wa, wb, ta, tb, stiff, dev, vel, sems
):
    layers, columns, sub = dims
    send_w = halves("width", ends[0])[2]
    send_t = halves("thick", ends[1])[2]
    copies = fetch((dev_hbm, vel_hbm, stiff_hbm), (dev, vel, stiff), sems)
    copies[0].wait()
    copies[1].wait()
    for c in range(9):
        ref, lead = (dev, (c,)) if c < 6 else (vel, (c - 6,))
        for t in range(layers):
            low = row_of(ref, (*lead, t), 0, columns, sub)
            high = row_of(ref, (*lead, t), columns - 1, columns, sub)
            wa[c, t], wb[c, t] = send_w(low, high)
        ta[c], tb[c] = send_t(ref[(*lead, 0)], ref[(*lead, layers - 1)])
    for copy in copies[2:]:
        copy.wait()


HALF = 0.5 * TIME_STEP


def inner_kernel(dims, dev, vel, ext, tau):
    layers, columns, sub = dims
    masks = edge_masks(sub)
    zero = jnp.zeros((sub, LANES), jnp.float32)
    for c in range(9):
        ref, lead = (dev, (c,)) if c < 6 else (vel, (c - 6,))
        for t in range(layers):
            for w in range(columns):
                ext[c, t + 1, w + 1] = row_of(ref, (*lead, t), w, columns, sub)
            ext[c, t + 1, 0] = zero
            ext[c, t + 1, columns + 1] = zero
        for w in range(columns):
            ext[c, 0, w + 1] = zero
            ext[c, layers + 1, w + 1] = zero

    def cell(t, w):
        def at(c, d, off):
            where = [t + 1, w + 1]
            where[d] = where[d] + off
            return ext[c, where[0], where[1]]

        s = [ext[c, t + 1, w + 1] for c in range(6)]
        u = [ext[6 + c, t + 1, w + 1] for c in range(3)]
        grad = [
            [HALF * (at(6 + i, j, 1) - at(6 + i, j, -1)) for j in range(2)]
            + [HALF * (after(u[i], masks) - before(u[i], masks))]
            for i in range(3)
        ]
        pos = [TIME_STEP * jnp.maximum(u[d], 0.0) for d in range(3)]
        neg = [TIME_STEP * jnp.minimum(u[d], 0.0) for d in range(3)]
        keep = (1.0 - TIME_STEP / RELAX_TIME) - (
            (pos[0] - neg[0]) + (pos[1] - neg[1]) + (pos[2] - neg[2])
        )
        bend = HALF * MOBILITY / RELAX_TIME
        scaled = [bend * s[c] for c in range(6)]
        turn = [[grad[i][k] - scaled[SLOT[i][k]] for k in range(3)] for i in range(3)]
        for p, (i, j) in enumerate(PAIRS):
            out = keep * s[p]
            for d in range(2):
                out = out + pos[d] * at(p, d, -1) - neg[d] * at(p, d, 1)
            out = out + pos[2] * before(s[p], masks) - neg[2] * after(s[p], masks)
            if i == j:
                more = grad[i][i]
                for k in range(3):
                    more = more + turn[i][k] * s[SLOT[k][i]]
                out = out + 2.0 * more
            else:
                out = out + (grad[i][j] + grad[j][i])
                for k in range(3):
                    out = out + turn[i][k] * s[SLOT[k][j]] + turn[j][k] * s[SLOT[k][i]]
            tau[p, t, w] = out

    def cells(step, carry):
        t, w = step // (columns // 2), step % (columns // 2)
        cell(t, 2 * w)
        cell(t, 2 * w + 1)
        return carry

    lax.fori_loop(0, layers * columns // 2, cells, 0)


def nodes(dims, tau, columns_of_nodes, put):
    layers, columns, sub = dims
    masks = edge_masks(sub)
    scale = 0.25 * MODULUS
    for w in columns_of_nodes:
        lower = None
        for t in range(layers + 1):
            level = []
            if t < layers:
                here = [tau[c, t, w] for c in range(6)] if w < columns else None
                back = [tau[c, t, w - 1] for c in range(6)] if w > 0 else None
                if here is None:
                    total, delta = back, [-x for x in back]
                elif back is None:
                    total = delta = here
                else:
                    total = [a + b for a, b in zip(here, back)]
                    delta = [a - b for a, b in zip(here, back)]
                for i in range(3):
                    m, q = delta[SLOT[i][1]], total[SLOT[i][2]]
                    level.append((total[SLOT[i][0]], m + q, m - q))
            for i in range(3):
                if t < layers:
                    x, y, z = level[i]
                    plus, minus = x + y, x + z
                    if t > 0:
                        plus, minus = plus + lower[i][0], minus + lower[i][1]
                else:
                    plus, minus = lower[i]
                put(i, t, w, scale * (plus + before(minus, masks)))
            lower = [(y - x, z - x) for x, y, z in level]


def correct(tau, ext, t, w, d, sign, halo):
    s = [ext[c, t + 1, w + 1] for c in range(6)]
    u = ext[6 + d, t + 1, w + 1]
    speed = TIME_STEP * (jnp.maximum(u, 0.0) if sign < 0 else -jnp.minimum(u, 0.0))
    h = [(sign * HALF) * halo[6 + i] for i in range(3)]
    q = [s[SLOT[d][j]] for j in range(3)]
    q[d] = q[d] + 1.0
    for p, (i, j) in enumerate(PAIRS):
        bent = 2.0 * (h[i] * q[i]) if i == j else h[i] * q[j] + h[j] * q[i]
        tau[p, t, w] = tau[p, t, w] + (speed * halo[p] + bent)


def side_kernel(dims, ends, tau_in, ext, wa, wb, tau):
    layers, columns, sub = dims
    w_low, w_high, _, _ = halves("width", ends[0])

    def side(t, carry):
        a, b = [wa[c, t] for c in range(9)], [wb[c, t] for c in range(9)]
        correct(tau, ext, t, 0, 1, -1.0, [w_low(x, y) for x, y in zip(a, b)])
        correct(tau, ext, t, columns - 1, 1, 1.0, [w_high(x, y) for x, y in zip(a, b)])
        return carry

    lax.fori_loop(0, layers, side, 0)


def outer_kernel(dims, ends, tau_in, ext, ta, tb, stiff, tau, part, sa, sb):
    layers, columns, sub = dims
    send_w = halves("width", ends[0])[2]
    t_low, t_high, _, _ = halves("thick", ends[1])
    for w in range(columns):
        a = [row_of(ta, (c,), w, columns, sub) for c in range(9)]
        b = [row_of(tb, (c,), w, columns, sub) for c in range(9)]
        correct(tau, ext, 0, w, 0, -1.0, [t_low(x, y) for x, y in zip(a, b)])
        correct(tau, ext, layers - 1, w, 0, 1.0, [t_high(x, y) for x, y in zip(a, b)])

    slot = {0: 0, 1: 1, columns - 1: 2, columns: 3}

    def put(i, t, w, value):
        part[i, t, slot[w]] = value

    nodes(dims, tau, slot, put)
    count = 2 * (layers + 1)
    for i in range(3):
        for t in range(layers + 1):
            for k in range(2):
                at = i * count + t * 2 + k
                sa[at], sb[at] = send_w(part[i, t, k], part[i, t, 2 + k])
    for t in range(layers):
        row = row_of(stiff, (t,), 0, columns, sub)
        sa[3 * count + t] = row
        sb[3 * count + t] = row


def middle_kernel(dims, ends, tau, part, stiff, mid, sa, sb):
    layers, columns, sub = dims
    send_t = halves("thick", ends[1])[2]

    def put(i, t, w, value):
        mid[i, t, w - 1] = value

    nodes(dims, tau, range(2, columns - 1), put)
    for i in range(3):
        for t in range(layers + 1):
            mid[i, t, 0] = part[i, t, 1]
            mid[i, t, columns - 2] = part[i, t, 2]
    inner = columns - 1
    for i in range(3):
        for k in range(2):
            for w in range(inner):
                at = (i * 2 + k) * inner + w
                sa[at], sb[at] = send_t(mid[i, k, w], mid[i, layers - 1 + k, w])
    for w in range(columns):
        row = row_of(stiff, (0,), w, columns, sub)
        sa[6 * inner + w] = row
        sb[6 * inner + w] = row


def emit_kernel(dims, tau, after_join, new, done):
    layers, columns, sub = dims
    done[...] = jnp.zeros_like(done)
    for c in range(6):
        for t in range(layers):
            for w in range(columns):
                new[c, t, pl.ds(w, sub, stride=columns), :] = tau[c, t, w]


def join_kernel(dims, ends, part, wa, wb, side, sa, sb):
    layers, columns, sub = dims
    w_low, w_high, _, has_high = halves("width", ends[0])
    send_t = halves("thick", ends[1])[2]
    count = 2 * (layers + 1)
    for i in range(3):
        for t in range(layers + 1):
            at = i * count + t * 2
            below = [w_low(wa[at + k], wb[at + k]) for k in range(2)]
            above = [w_high(wa[at + k], wb[at + k]) for k in range(2)]
            side[i, t, 0] = below[0]
            side[i, t, 1] = part[i, t, 0] + below[1]
            side[i, t, 2] = jnp.where(has_high, part[i, t, 3] + above[0], 0.0)
            side[i, t, 3] = above[1]
    for i in range(3):
        for k in range(2):
            for w in range(4):
                at = (i * 2 + k) * 4 + w
                sa[at], sb[at] = send_t(side[i, k, w], side[i, layers - 1 + k, w])


def krylov_part(dims, ends, late, ext, img, stiff, top_stiff, right_stiff):
    layers, columns, sub = dims
    has_right = halves("width", ends[0])[3]
    has_top = halves("thick", ends[1])[3]
    masks = edge_masks(sub)
    zero = jnp.zeros((sub, LANES), jnp.float32)

    def stage(t, w):
        if 2 <= w <= columns - 2:
            return 0
        rim = 2 if w in (0, columns) else 1
        return 0 if rim <= t <= layers - rim else 1

    def apply(i, t, w, diagonal):
        here = ext[i, t + 1, w + 1]
        beside = ext[i, t, w + 1] + ext[i, t + 2, w + 1]
        beside = beside + (ext[i, t + 1, w] + ext[i, t + 1, w + 2])
        near, far = before(here, masks), after(here, masks)
        return here, diagonal * here - (beside + (near + far))

    for t in range(layers):
        if stage(t, columns) == late:
            d = 6.0 + right_stiff(t)
            for i in range(3):
                _, g = apply(i, t, columns, d)
                img[i, t, columns] = jnp.where(has_right, g, 0.0)
    for w in range(columns):
        if stage(layers, w) == late:
            d = 6.0 + top_stiff(w)
            for i in range(3):
                _, g = apply(i, layers, w, d)
                img[i, layers, w] = jnp.where(has_top, g, 0.0)
    m0 = m1 = m2 = m3 = me = zero
    for t in range(layers):
        for w in range(columns):
            if stage(t, w) == late:
                d = 6.0 + row_of(stiff, (t,), w, columns, sub)
                square = zero
                for i in range(3):
                    f, g = apply(i, t, w, d)
                    img[i, t, w] = g
                    m0, m1 = m0 + f * f, m1 + f * g
                    square = square + g * g
                    me = me + g * after(g, masks)
                m2, m3 = m2 + square, m3 + d * square
    for t in range(layers):
        for w in range(columns):
            beside = [p for p in ((t + 1, w), (t, w + 1)) if max(stage(t, w), stage(*p)) == late]
            for i in range(3):
                if beside:
                    total = img[i, beside[0][0], beside[0][1]]
                    for p in beside[1:]:
                        total = total + img[i, p[0], p[1]]
                    me = me + img[i, t, w] * total
    return m0, m1, m2, m3, me


def early_kernel(dims, ends, mid, side, mb, ma, wa, wb, stiff, ext, img, held):
    layers, columns, sub = dims
    w_high = halves("width", ends[0])[1]
    t_low, t_high, _, has_top = halves("thick", ends[1])
    inner = columns - 1
    for i in range(3):
        for at in range(inner):
            a = [ma[(i * 2 + k) * inner + at] for k in range(2)]
            b = [mb[(i * 2 + k) * inner + at] for k in range(2)]
            below = [t_low(x, y) for x, y in zip(a, b)]
            above = [t_high(x, y) for x, y in zip(a, b)]
            w = at + 2
            ext[i, 0, w] = below[0]
            ext[i, 1, w] = mid[i, 0, at] + below[1]
            for t in range(1, layers):
                ext[i, t + 1, w] = mid[i, t, at]
            ext[i, layers + 1, w] = jnp.where(has_top, mid[i, layers, at] + above[0], 0.0)
            ext[i, layers + 2, w] = above[1]
        for at, w in enumerate((0, 1, columns + 1, columns + 2)):
            for t in range(1, layers):
                ext[i, t + 1, w] = side[i, t, at]
    count = 6 * (layers + 1)
    sums = krylov_part(
        dims, ends, 0, ext, img, stiff,
        lambda w: t_high(ma[6 * inner + w], mb[6 * inner + w]),
        lambda t: w_high(wa[count + t], wb[count + t]),
    )
    for k, m in enumerate(sums):
        held[k] = m


def late_kernel(
    dims, ends, ext_in, img_in, held, side, jb, ja, mb, ma, wa, wb, stiff, after_emit, ext, img, sums
):
    layers, columns, sub = dims
    w_high = halves("width", ends[0])[1]
    t_low, t_high, _, has_top = halves("thick", ends[1])
    inner = columns - 1
    for i in range(3):
        for at, w in enumerate((0, 1, columns + 1, columns + 2)):
            a = [ja[(i * 2 + k) * 4 + at] for k in range(2)]
            b = [jb[(i * 2 + k) * 4 + at] for k in range(2)]
            below = [t_low(x, y) for x, y in zip(a, b)]
            above = [t_high(x, y) for x, y in zip(a, b)]
            ext[i, 0, w] = below[0]
            ext[i, 1, w] = side[i, 0, at] + below[1]
            ext[i, layers + 1, w] = jnp.where(has_top, side[i, layers, at] + above[0], 0.0)
            ext[i, layers + 2, w] = above[1]
    count = 6 * (layers + 1)
    more = krylov_part(
        dims, ends, 1, ext, img, stiff,
        lambda w: t_high(ma[6 * inner + w], mb[6 * inner + w]),
        lambda t: w_high(wa[count + t], wb[count + t]),
    )
    m0, m1, m2, m3, me = [held[k] + m for k, m in enumerate(more)]
    m3 = m3 - 2.0 * me
    lane = lax.broadcasted_iota(jnp.int32, (1, LANES), 1)
    line = jnp.zeros((1, LANES), jnp.float32)
    for k, m in enumerate((m0, m1, m2, m3)):
        line = jnp.where(lane == k, jnp.sum(m, keepdims=True), line)
    sums[...] = jnp.broadcast_to(line[None], sums.shape)


def finish_kernel(dims, sums, force, image, out):
    layers, columns, sub = dims
    line = jnp.sum(sums[...], axis=0)
    lane = lax.broadcasted_iota(jnp.int32, (1, LANES), 1)
    m0, m1, m2, m3 = [
        jnp.sum(jnp.where(lane == k, line, 0.0), axis=1, keepdims=True) for k in range(4)
    ]
    a1 = m0 / m1
    left = a1 * a1 * m2 - m0
    grow = 1.0 + left / m0
    a2 = left / (grow * grow * m1 - 2.0 * grow * a1 * m2 + a1 * a1 * m3)
    c0 = jnp.broadcast_to(a1 + a2 * grow, (sub, LANES))
    c1 = jnp.broadcast_to(a1 * a2, (sub, LANES))
    for i in range(3):
        for t in range(layers):
            for w in range(columns):
                out[i, t, pl.ds(w, sub, stride=columns), :] = (
                    c0 * force[i, t + 1, w + 1] - c1 * image[i, t, w]
                )


def call(
    kernel, shapes, scratch=(), hbm=(), count=0, copies=0, aliases=None, cost=None, work=0
):
    anywhere, local = pl.BlockSpec(memory_space=pl.ANY), pl.BlockSpec(memory_space=pltpu.VMEM)
    extra = [pltpu.SemaphoreType.DMA((copies,))] if copies else []
    more = {}
    if cost is not None:
        more["cost_estimate"] = pl.CostEstimate(flops=work, transcendentals=0, bytes_accessed=cost)
    return pl.pallas_call(
        kernel,
        out_shape=[jax.ShapeDtypeStruct(s, jnp.float32) for s in shapes],
        in_specs=[anywhere if k in hbm else local for k in range(count)],
        scratch_shapes=[pltpu.VMEM(s, jnp.float32) for s in scratch] + extra,
        input_output_aliases=aliases or {},
        compiler_params=pltpu.CompilerParams(vmem_limit_bytes=VMEM_LIMIT),
        **more,
    )


def on_device(ends, deviation, velocity, stiffness):
    _, layers, columns, length = deviation.shape
    sub = length // LANES
    dims = (layers, columns, sub)
    rows = columns * sub
    tile = (sub, LANES)
    w_first, w_second, t_first, t_second, t_across, t_missing = swap_pairs(*ends)
    dev, vel, stiff = as_tiles(deviation), as_tiles(velocity), as_tiles(stiffness)

    wa, wb, ta, tb, stiff, dev, vel = call(
        functools.partial(pack_kernel, dims, ends),
        [(9, layers, *tile)] * 2
        + [(9, rows, LANES)] * 2
        + [(layers, rows, LANES), (6, layers, rows, LANES), (3, layers, rows, LANES)],
        hbm=(0, 1, 2), count=3, copies=3,
    )(*[pltpu.with_memory_space_constraint(x, pltpu.HBM) for x in (dev, vel, stiff)])
    tb = swap(tb, t_missing)
    wb = swap(wb, w_second)
    wa = swap(wa, w_first)
    ta = swap(ta, t_first)

    ext, tau = call(
        functools.partial(inner_kernel, dims),
        [(9, layers + 2, columns + 2, *tile), (6, layers, columns, *tile)],
        count=2, cost=12 * 1024 * 1024,
    )(dev, vel)

    (tau,) = call(
        functools.partial(side_kernel, dims, ends),
        [(6, layers, columns, *tile)],
        count=4, aliases={0: 0}, cost=1024 * 1024, work=10**10,
    )(tau, ext, wa, wb)

    face = 6 * (layers + 1) + layers
    tau, part, sa, sb = call(
        functools.partial(outer_kernel, dims, ends),
        [(6, layers, columns, *tile), (3, layers + 1, 4, *tile)] + [(face, *tile)] * 2,
        count=5, aliases={0: 0},
    )(tau, ext, ta, tb, stiff)
    wb = swap(sb, w_second)
    wa = swap(sa, w_first)

    broad = 6 * (columns - 1) + columns
    mid, sa, sb = call(
        functools.partial(middle_kernel, dims, ends),
        [(3, layers + 1, columns - 1, *tile)] + [(broad, *tile)] * 2,
        count=3, cost=2 * 1024 * 1024,
    )(tau, part, stiff)
    mb = swap(sb, t_across)
    ma = swap(sa, t_first)

    side, sa, sb = call(
        functools.partial(join_kernel, dims, ends),
        [(3, layers + 1, 4, *tile)] + [(24, *tile)] * 2,
        count=3,
    )(part, wa, wb)
    jb = swap(sb, t_second)
    ja = swap(sa, t_first)

    new, done = call(
        functools.partial(emit_kernel, dims), [(6, layers, rows, LANES), tile],
        hbm=(1,), count=2, cost=6 * 1024 * 1024,
    )(tau, side)

    around = [(3, layers + 3, columns + 3, *tile), (3, layers + 1, columns + 1, *tile)]
    force, image, held = call(
        functools.partial(early_kernel, dims, ends),
        around + [(5, *tile)],
        count=7, cost=2 * 1024 * 1024,
    )(mid, side, mb, ma, wa, wb, stiff)
    force, image, sums = call(
        functools.partial(late_kernel, dims, ends),
        around + [(ends[0] * ends[1], 1, LANES)],
        count=12, aliases={0: 0, 1: 1},
    )(force, image, held, side, jb, ja, mb, ma, wa, wb, stiff, done)
    sums = lax.all_to_all(sums, AXES, 0, 0, tiled=True)

    (out,) = call(
        functools.partial(finish_kernel, dims), [(3, layers, rows, LANES)], count=3
    )(sums, force, image)
    return from_tiles(new, columns), from_tiles(out, columns)


def solution(mesh):
    placed = (
        P(None, "thick", "width", None),
        P(None, "thick", "width", None),
        P("thick", "width", None),
    )
    ends = (mesh.shape["width"], mesh.shape["thick"])
    return jax.shard_map(
        functools.partial(on_device, ends),
        mesh=mesh,
        in_specs=placed,
        out_specs=(P(None, "thick", "width", None), P(None, "thick", "width", None)),
        check_vma=False,
    )
```

```python
import functools

import jax
import jax.numpy as jnp
from jax import lax
from jax.experimental import pallas as pl
from jax.experimental.pallas import tpu as pltpu
from jax.sharding import PartitionSpec as P

TIME_STEP = 0.1
RELAX_TIME = 1.0
MOBILITY = 0.3
MODULUS = 10.0
LANES = 128
AXES = ("width", "thick")
PAIRS = ((0, 0), (1, 1), (2, 2), (0, 1), (0, 2), (1, 2))
SLOT = ((0, 3, 4), (3, 1, 5), (4, 5, 2))
VMEM_LIMIT = 40 * 1024 * 1024


def swap_pairs(wide, thick):
    def flat(fn):
        return [
            (w * thick + t, fn(w, t)[0] * thick + fn(w, t)[1])
            for w in range(wide)
            for t in range(thick)
        ]

    def width_second(w, t):
        return (w, t ^ 1) if w in (0, wide - 1) else (((w - 1) ^ 1) + 1, t)

    def thick_second(w, t):
        return (w ^ 2, t) if t in (0, thick - 1) else (w, ((t - 1) ^ 1) + 1)

    def thick_across(w, t):
        return (w, thick - 1 - t) if t in (0, thick - 1) else (w, ((t - 1) ^ 1) + 1)

    return (
        flat(lambda w, t: (w ^ 1, t)),
        flat(width_second),
        flat(lambda w, t: (w, t ^ 1)),
        flat(thick_second),
        flat(thick_across),
        [p for p in flat(thick_across) if p[0] % thick not in (0, thick - 1)],
    )


def swap(value, pairs):
    return lax.ppermute(value, AXES, pairs)


def as_tiles(x):
    *lead, w, length = x.shape
    x = x.reshape(*lead, w, length // LANES, LANES)
    return jnp.swapaxes(x, -3, -2).reshape(*lead, length // LANES * w, LANES)


def from_tiles(x, w):
    *lead, rows, lanes = x.shape
    x = x.reshape(*lead, rows // w, w, lanes)
    return jnp.swapaxes(x, -3, -2).reshape(*lead, w, rows // w * lanes)


def row_of(ref, lead, w, columns, sub):
    return ref[(*lead, pl.ds(w, sub, stride=columns), slice(None))]


def edge_masks(sub):
    lane = lax.broadcasted_iota(jnp.int32, (sub, LANES), 1)
    row = lax.broadcasted_iota(jnp.int32, (sub, LANES), 0)
    first, last = lane == 0, lane == LANES - 1
    return first, first & (row == 0), last, last & (row == sub - 1)


def before(x, masks):
    first, corner = masks[0], masks[1]
    near = pltpu.roll(x, 1, axis=1)
    far = pltpu.roll(near, 1, axis=0)
    return jnp.where(corner, 0.0, jnp.where(first, far, near))


def after(x, masks):
    last, corner = masks[2], masks[3]
    sub = x.shape[0]
    near = pltpu.roll(x, LANES - 1, axis=1)
    far = pltpu.roll(near, sub - 1, axis=0)
    return jnp.where(corner, 0.0, jnp.where(last, far, near))


def halves(axis, end):
    at = lax.axis_index(axis)
    even = at % 2 == 0
    has_low, has_high = at > 0, at < end - 1

    def low(first, second):
        return jnp.where(has_low, jnp.where(even, second, first), 0.0)

    def high(first, second):
        return jnp.where(has_high, jnp.where(even, first, second), 0.0)

    def send(low_face, high_face):
        return jnp.where(even, high_face, low_face), jnp.where(even, low_face, high_face)

    return low, high, send, has_high


def fetch(sources, targets, sems):
    copies = []
    for source, target in zip(sources, targets):
        copies.append(pltpu.make_async_copy(source, target, sems.at[len(copies)]))
    for copy in copies:
        copy.start()
    return copies


def pack_kernel(
    dims, ends, dev_hbm, vel_hbm, stiff_hbm, wa, wb, ta, tb, stiff, dev, vel, sems
):
    layers, columns, sub = dims
    send_w = halves("width", ends[0])[2]
    send_t = halves("thick", ends[1])[2]
    copies = fetch((dev_hbm, vel_hbm, stiff_hbm), (dev, vel, stiff), sems)
    copies[0].wait()
    copies[1].wait()
    for c in range(9):
        ref, lead = (dev, (c,)) if c < 6 else (vel, (c - 6,))
        for t in range(layers):
            low = row_of(ref, (*lead, t), 0, columns, sub)
            high = row_of(ref, (*lead, t), columns - 1, columns, sub)
            wa[c, t], wb[c, t] = send_w(low, high)
        ta[c], tb[c] = send_t(ref[(*lead, 0)], ref[(*lead, layers - 1)])
    for copy in copies[2:]:
        copy.wait()


HALF = 0.5 * TIME_STEP


def inner_kernel(dims, dev, vel, ext, tau):
    layers, columns, sub = dims
    masks = edge_masks(sub)
    zero = jnp.zeros((sub, LANES), jnp.float32)
    for c in range(9):
        ref, lead = (dev, (c,)) if c < 6 else (vel, (c - 6,))
        for t in range(layers):
            for w in range(columns):
                ext[c, t + 1, w + 1] = row_of(ref, (*lead, t), w, columns, sub)
            ext[c, t + 1, 0] = zero
            ext[c, t + 1, columns + 1] = zero
        for w in range(columns):
            ext[c, 0, w + 1] = zero
            ext[c, layers + 1, w + 1] = zero

    def cell(t, w):
        def at(c, d, off):
            where = [t + 1, w + 1]
            where[d] = where[d] + off
            return ext[c, where[0], where[1]]

        s = [ext[c, t + 1, w + 1] for c in range(6)]
        u = [ext[6 + c, t + 1, w + 1] for c in range(3)]
        grad = [
            [HALF * (at(6 + i, j, 1) - at(6 + i, j, -1)) for j in range(2)]
            + [HALF * (after(u[i], masks) - before(u[i], masks))]
            for i in range(3)
        ]
        pos = [TIME_STEP * jnp.maximum(u[d], 0.0) for d in range(3)]
        neg = [TIME_STEP * jnp.minimum(u[d], 0.0) for d in range(3)]
        keep = (1.0 - TIME_STEP / RELAX_TIME) - (
            (pos[0] - neg[0]) + (pos[1] - neg[1]) + (pos[2] - neg[2])
        )
        bend = HALF * MOBILITY / RELAX_TIME
        scaled = [bend * s[c] for c in range(6)]
        turn = [[grad[i][k] - scaled[SLOT[i][k]] for k in range(3)] for i in range(3)]
        for p, (i, j) in enumerate(PAIRS):
            out = keep * s[p]
            for d in range(2):
                out = out + pos[d] * at(p, d, -1) - neg[d] * at(p, d, 1)
            out = out + pos[2] * before(s[p], masks) - neg[2] * after(s[p], masks)
            if i == j:
                more = grad[i][i]
                for k in range(3):
                    more = more + turn[i][k] * s[SLOT[k][i]]
                out = out + 2.0 * more
            else:
                out = out + (grad[i][j] + grad[j][i])
                for k in range(3):
                    out = out + turn[i][k] * s[SLOT[k][j]] + turn[j][k] * s[SLOT[k][i]]
            tau[p, t, w] = out

    def cells(step, carry):
        t, w = step // (columns // 2), step % (columns // 2)
        cell(t, 2 * w)
        cell(t, 2 * w + 1)
        return carry

    lax.fori_loop(0, layers * columns // 2, cells, 0)


def nodes(dims, tau, columns_of_nodes, put):
    layers, columns, sub = dims
    masks = edge_masks(sub)
    scale = 0.25 * MODULUS
    for w in columns_of_nodes:
        lower = None
        for t in range(layers + 1):
            level = []
            if t < layers:
                here = [tau[c, t, w] for c in range(6)] if w < columns else None
                back = [tau[c, t, w - 1] for c in range(6)] if w > 0 else None
                if here is None:
                    total, delta = back, [-x for x in back]
                elif back is None:
                    total = delta = here
                else:
                    total = [a + b for a, b in zip(here, back)]
                    delta = [a - b for a, b in zip(here, back)]
                for i in range(3):
                    m, q = delta[SLOT[i][1]], total[SLOT[i][2]]
                    level.append((total[SLOT[i][0]], m + q, m - q))
            for i in range(3):
                if t < layers:
                    x, y, z = level[i]
                    plus, minus = x + y, x + z
                    if t > 0:
                        plus, minus = plus + lower[i][0], minus + lower[i][1]
                else:
                    plus, minus = lower[i]
                put(i, t, w, scale * (plus + before(minus, masks)))
            lower = [(y - x, z - x) for x, y, z in level]


def correct(tau, ext, t, w, d, sign, halo):
    s = [ext[c, t + 1, w + 1] for c in range(6)]
    u = ext[6 + d, t + 1, w + 1]
    speed = TIME_STEP * (jnp.maximum(u, 0.0) if sign < 0 else -jnp.minimum(u, 0.0))
    h = [(sign * HALF) * halo[6 + i] for i in range(3)]
    q = [s[SLOT[d][j]] for j in range(3)]
    q[d] = q[d] + 1.0
    for p, (i, j) in enumerate(PAIRS):
        bent = 2.0 * (h[i] * q[i]) if i == j else h[i] * q[j] + h[j] * q[i]
        tau[p, t, w] = tau[p, t, w] + (speed * halo[p] + bent)


def side_kernel(dims, ends, tau_in, ext, wa, wb, tau):
    layers, columns, sub = dims
    w_low, w_high, _, _ = halves("width", ends[0])

    def side(t, carry):
        a, b = [wa[c, t] for c in range(9)], [wb[c, t] for c in range(9)]
        correct(tau, ext, t, 0, 1, -1.0, [w_low(x, y) for x, y in zip(a, b)])
        correct(tau, ext, t, columns - 1, 1, 1.0, [w_high(x, y) for x, y in zip(a, b)])
        return carry

    lax.fori_loop(0, layers, side, 0)


def outer_kernel(dims, ends, tau_in, ext, ta, tb, stiff, tau, part, sa, sb):
    layers, columns, sub = dims
    send_w = halves("width", ends[0])[2]
    t_low, t_high, _, _ = halves("thick", ends[1])
    for w in range(columns):
        a = [row_of(ta, (c,), w, columns, sub) for c in range(9)]
        b = [row_of(tb, (c,), w, columns, sub) for c in range(9)]
        correct(tau, ext, 0, w, 0, -1.0, [t_low(x, y) for x, y in zip(a, b)])
        correct(tau, ext, layers - 1, w, 0, 1.0, [t_high(x, y) for x, y in zip(a, b)])

    slot = {0: 0, 1: 1, columns - 1: 2, columns: 3}

    def put(i, t, w, value):
        part[i, t, slot[w]] = value

    nodes(dims, tau, slot, put)
    count = 2 * (layers + 1)
    for i in range(3):
        for t in range(layers + 1):
            for k in range(2):
                at = i * count + t * 2 + k
                sa[at], sb[at] = send_w(part[i, t, k], part[i, t, 2 + k])
    for t in range(layers):
        row = row_of(stiff, (t,), 0, columns, sub)
        sa[3 * count + t] = row
        sb[3 * count + t] = row


def middle_kernel(dims, ends, tau, part, stiff, mid, sa, sb):
    layers, columns, sub = dims
    send_t = halves("thick", ends[1])[2]

    def put(i, t, w, value):
        mid[i, t, w - 1] = value

    nodes(dims, tau, range(2, columns - 1), put)
    for i in range(3):
        for t in range(layers + 1):
            mid[i, t, 0] = part[i, t, 1]
            mid[i, t, columns - 2] = part[i, t, 2]
    inner = columns - 1
    for i in range(3):
        for k in range(2):
            for w in range(inner):
                at = (i * 2 + k) * inner + w
                sa[at], sb[at] = send_t(mid[i, k, w], mid[i, layers - 1 + k, w])
    for w in range(columns):
        row = row_of(stiff, (0,), w, columns, sub)
        sa[6 * inner + w] = row
        sb[6 * inner + w] = row


def emit_kernel(dims, tau, after_join, new, done):
    layers, columns, sub = dims
    done[...] = jnp.zeros_like(done)
    for c in range(6):
        for t in range(layers):
            for w in range(columns):
                new[c, t, pl.ds(w, sub, stride=columns), :] = tau[c, t, w]


CORNERS = ((0, 0), (0, 1), (0, 2), (0, 3), (1, 1), (1, 2))


def join_kernel(dims, ends, part, wa, wb, side, sa, sb):
    layers, columns, sub = dims
    w_low, w_high, _, has_high = halves("width", ends[0])
    send_t = halves("thick", ends[1])[2]
    count = 2 * (layers + 1)
    for i in range(3):
        for t in range(layers + 1):
            at = i * count + t * 2
            below = [w_low(wa[at + k], wb[at + k]) for k in range(2)]
            above = [w_high(wa[at + k], wb[at + k]) for k in range(2)]
            side[i, t, 0] = below[0]
            side[i, t, 1] = part[i, t, 0] + below[1]
            side[i, t, 2] = jnp.where(has_high, part[i, t, 3] + above[0], 0.0)
            side[i, t, 3] = above[1]
    for i in range(3):
        for q, (depth, w) in enumerate(CORNERS):
            at = i * len(CORNERS) + q
            sa[at], sb[at] = send_t(side[i, depth, w], side[i, layers - depth, w])


def krylov_part(dims, ends, late, ext, img, stiff, top_stiff, right_stiff):
    layers, columns, sub = dims
    has_right = halves("width", ends[0])[3]
    has_top = halves("thick", ends[1])[3]
    masks = edge_masks(sub)
    zero = jnp.zeros((sub, LANES), jnp.float32)

    def stage(t, w):
        if 2 <= w <= columns - 2:
            return 0
        rim = 2 if w in (0, columns) else 1
        return 0 if rim <= t <= layers - rim else 1

    def apply(i, t, w, diagonal):
        here = ext[i, t + 1, w + 1]
        beside = ext[i, t, w + 1] + ext[i, t + 2, w + 1]
        beside = beside + (ext[i, t + 1, w] + ext[i, t + 1, w + 2])
        near, far = before(here, masks), after(here, masks)
        return here, diagonal * here - (beside + (near + far))

    for t in range(layers):
        if stage(t, columns) == late:
            d = 6.0 + right_stiff(t)
            for i in range(3):
                _, g = apply(i, t, columns, d)
                img[i, t, columns] = jnp.where(has_right, g, 0.0)
    for w in range(columns):
        if stage(layers, w) == late:
            d = 6.0 + top_stiff(w)
            for i in range(3):
                _, g = apply(i, layers, w, d)
                img[i, layers, w] = jnp.where(has_top, g, 0.0)
    m0 = m1 = m2 = m3 = me = zero
    for t in range(layers):
        for w in range(columns):
            if stage(t, w) == late:
                d = 6.0 + row_of(stiff, (t,), w, columns, sub)
                square = zero
                for i in range(3):
                    f, g = apply(i, t, w, d)
                    img[i, t, w] = g
                    m0, m1 = m0 + f * f, m1 + f * g
                    square = square + g * g
                    me = me + g * after(g, masks)
                m2, m3 = m2 + square, m3 + d * square
    for t in range(layers):
        for w in range(columns):
            beside = [p for p in ((t + 1, w), (t, w + 1)) if max(stage(t, w), stage(*p)) == late]
            for i in range(3):
                if beside:
                    total = img[i, beside[0][0], beside[0][1]]
                    for p in beside[1:]:
                        total = total + img[i, p[0], p[1]]
                    me = me + img[i, t, w] * total
    return m0, m1, m2, m3, me


def early_kernel(dims, ends, mid, side, mb, ma, wa, wb, stiff, ext, img, held):
    layers, columns, sub = dims
    w_high = halves("width", ends[0])[1]
    t_low, t_high, _, has_top = halves("thick", ends[1])
    inner = columns - 1
    for i in range(3):
        for at in range(inner):
            a = [ma[(i * 2 + k) * inner + at] for k in range(2)]
            b = [mb[(i * 2 + k) * inner + at] for k in range(2)]
            below = [t_low(x, y) for x, y in zip(a, b)]
            above = [t_high(x, y) for x, y in zip(a, b)]
            w = at + 2
            ext[i, 0, w] = below[0]
            ext[i, 1, w] = mid[i, 0, at] + below[1]
            for t in range(1, layers):
                ext[i, t + 1, w] = mid[i, t, at]
            ext[i, layers + 1, w] = jnp.where(has_top, mid[i, layers, at] + above[0], 0.0)
            ext[i, layers + 2, w] = above[1]
        for at, w in enumerate((0, 1, columns + 1, columns + 2)):
            for t in range(1, layers):
                ext[i, t + 1, w] = side[i, t, at]
    count = 6 * (layers + 1)
    sums = krylov_part(
        dims, ends, 0, ext, img, stiff,
        lambda w: t_high(ma[6 * inner + w], mb[6 * inner + w]),
        lambda t: w_high(wa[count + t], wb[count + t]),
    )
    for k, m in enumerate(sums):
        held[k] = m


def late_kernel(
    dims, ends, ext_in, img_in, held, side, jb, ja, mb, ma, wa, wb, stiff, after_emit, ext, img, sums
):
    layers, columns, sub = dims
    w_high = halves("width", ends[0])[1]
    t_low, t_high, _, has_top = halves("thick", ends[1])
    inner = columns - 1
    for i in range(3):
        for q, (depth, at) in enumerate(CORNERS):
            a, b = ja[i * len(CORNERS) + q], jb[i * len(CORNERS) + q]
            below, above = t_low(a, b), t_high(a, b)
            w = (0, 1, columns + 1, columns + 2)[at]
            if depth == 0:
                ext[i, 1, w] = side[i, 0, at] + below
                ext[i, layers + 1, w] = jnp.where(has_top, side[i, layers, at] + above, 0.0)
            else:
                ext[i, 0, w] = below
                ext[i, layers + 2, w] = above
    count = 6 * (layers + 1)
    more = krylov_part(
        dims, ends, 1, ext, img, stiff,
        lambda w: t_high(ma[6 * inner + w], mb[6 * inner + w]),
        lambda t: w_high(wa[count + t], wb[count + t]),
    )
    m0, m1, m2, m3, me = [held[k] + m for k, m in enumerate(more)]
    m3 = m3 - 2.0 * me
    lane = lax.broadcasted_iota(jnp.int32, (1, LANES), 1)
    line = jnp.zeros((1, LANES), jnp.float32)
    for k, m in enumerate((m0, m1, m2, m3)):
        line = jnp.where(lane == k, jnp.sum(m, keepdims=True), line)
    sums[...] = jnp.broadcast_to(line[None], sums.shape)


def finish_kernel(dims, sums, force, image, out):
    layers, columns, sub = dims
    line = jnp.sum(sums[...], axis=0)
    lane = lax.broadcasted_iota(jnp.int32, (1, LANES), 1)
    m0, m1, m2, m3 = [
        jnp.sum(jnp.where(lane == k, line, 0.0), axis=1, keepdims=True) for k in range(4)
    ]
    a1 = m0 / m1
    left = a1 * a1 * m2 - m0
    grow = 1.0 + left / m0
    a2 = left / (grow * grow * m1 - 2.0 * grow * a1 * m2 + a1 * a1 * m3)
    c0 = jnp.broadcast_to(a1 + a2 * grow, (sub, LANES))
    c1 = jnp.broadcast_to(a1 * a2, (sub, LANES))
    for i in range(3):
        for t in range(layers):
            for w in range(columns):
                out[i, t, pl.ds(w, sub, stride=columns), :] = (
                    c0 * force[i, t + 1, w + 1] - c1 * image[i, t, w]
                )


def call(
    kernel, shapes, scratch=(), hbm=(), count=0, copies=0, aliases=None, cost=None, work=0
):
    anywhere, local = pl.BlockSpec(memory_space=pl.ANY), pl.BlockSpec(memory_space=pltpu.VMEM)
    extra = [pltpu.SemaphoreType.DMA((copies,))] if copies else []
    more = {}
    if cost is not None:
        more["cost_estimate"] = pl.CostEstimate(flops=work, transcendentals=0, bytes_accessed=cost)
    return pl.pallas_call(
        kernel,
        out_shape=[jax.ShapeDtypeStruct(s, jnp.float32) for s in shapes],
        in_specs=[anywhere if k in hbm else local for k in range(count)],
        scratch_shapes=[pltpu.VMEM(s, jnp.float32) for s in scratch] + extra,
        input_output_aliases=aliases or {},
        compiler_params=pltpu.CompilerParams(vmem_limit_bytes=VMEM_LIMIT),
        **more,
    )


def on_device(ends, deviation, velocity, stiffness):
    _, layers, columns, length = deviation.shape
    sub = length // LANES
    dims = (layers, columns, sub)
    rows = columns * sub
    tile = (sub, LANES)
    w_first, w_second, t_first, t_second, t_across, t_missing = swap_pairs(*ends)
    dev, vel, stiff = as_tiles(deviation), as_tiles(velocity), as_tiles(stiffness)

    wa, wb, ta, tb, stiff, dev, vel = call(
        functools.partial(pack_kernel, dims, ends),
        [(9, layers, *tile)] * 2
        + [(9, rows, LANES)] * 2
        + [(layers, rows, LANES), (6, layers, rows, LANES), (3, layers, rows, LANES)],
        hbm=(0, 1, 2), count=3, copies=3,
    )(*[pltpu.with_memory_space_constraint(x, pltpu.HBM) for x in (dev, vel, stiff)])
    tb = swap(tb, t_missing)
    wb = swap(wb, w_second)
    wa = swap(wa, w_first)
    ta = swap(ta, t_first)

    ext, tau = call(
        functools.partial(inner_kernel, dims),
        [(9, layers + 2, columns + 2, *tile), (6, layers, columns, *tile)],
        count=2, cost=12 * 1024 * 1024,
    )(dev, vel)

    (tau,) = call(
        functools.partial(side_kernel, dims, ends),
        [(6, layers, columns, *tile)],
        count=4, aliases={0: 0}, cost=1024 * 1024, work=10**10,
    )(tau, ext, wa, wb)

    face = 6 * (layers + 1) + layers
    tau, part, sa, sb = call(
        functools.partial(outer_kernel, dims, ends),
        [(6, layers, columns, *tile), (3, layers + 1, 4, *tile)] + [(face, *tile)] * 2,
        count=5, aliases={0: 0},
    )(tau, ext, ta, tb, stiff)
    wb = swap(sb, w_second)
    wa = swap(sa, w_first)

    broad = 6 * (columns - 1) + columns
    mid, sa, sb = call(
        functools.partial(middle_kernel, dims, ends),
        [(3, layers + 1, columns - 1, *tile)] + [(broad, *tile)] * 2,
        count=3, cost=2 * 1024 * 1024,
    )(tau, part, stiff)
    mb = swap(sb, t_missing)
    ma = swap(sa, t_first)

    side, sa, sb = call(
        functools.partial(join_kernel, dims, ends),
        [(3, layers + 1, 4, *tile)] + [(3 * len(CORNERS), *tile)] * 2,
        count=3,
    )(part, wa, wb)
    jb = swap(sb, t_second)
    ja = swap(sa, t_first)

    new, done = call(
        functools.partial(emit_kernel, dims), [(6, layers, rows, LANES), tile],
        hbm=(1,), count=2, cost=6 * 1024 * 1024,
    )(tau, side)

    around = [(3, layers + 3, columns + 3, *tile), (3, layers + 1, columns + 1, *tile)]
    force, image, held = call(
        functools.partial(early_kernel, dims, ends),
        around + [(5, *tile)],
        count=7, cost=2 * 1024 * 1024,
    )(mid, side, mb, ma, wa, wb, stiff)
    force, image, sums = call(
        functools.partial(late_kernel, dims, ends),
        around + [(ends[0] * ends[1], 1, LANES)],
        count=12, aliases={0: 0, 1: 1},
    )(force, image, held, side, jb, ja, mb, ma, wa, wb, stiff, done)
    sums = lax.all_to_all(sums, AXES, 0, 0, tiled=True)

    (out,) = call(
        functools.partial(finish_kernel, dims), [(3, layers, rows, LANES)], count=3
    )(sums, force, image)
    return from_tiles(new, columns), from_tiles(out, columns)


def solution(mesh):
    placed = (
        P(None, "thick", "width", None),
        P(None, "thick", "width", None),
        P("thick", "width", None),
    )
    ends = (mesh.shape["width"], mesh.shape["thick"])
    return jax.shard_map(
        functools.partial(on_device, ends),
        mesh=mesh,
        in_specs=placed,
        out_specs=(P(None, "thick", "width", None), P(None, "thick", "width", None)),
        check_vma=False,
    )
```
